32 devices in a mesh: expert: 8 (over z, y), shard: 4 (over x, core).
Axes of the slice: x: 2, y: 2, z: 4, core: 2. Of those that a mesh axis runs over, the one named last changes fastest.
Arguments:
- tokens: bfloat16 [2, 4096, 2048], P(None, ('expert', 'shard')), may hold values from -6 to 6
- cotangent: bfloat16 [2, 4096, 2048], P(None, ('expert', 'shard')), may hold values from -6 to 6
- qkv_weight: bfloat16 [2048, 6144], replicated, may hold values from -0.125 to 0.125
- out_weight: bfloat16 [2048, 2048], replicated, may hold values from -1.75 to 1.75
- router_weight: bfloat16 [2048, 16], replicated, may hold values from -0.0625 to 0.0625
- attn_gain: float32 [2048], replicated, may hold values from 0.5 to 1.5
- moe_gain: float32 [2048], replicated, may hold values from 0.5 to 1.5
- head_gains: float32 [256], replicated, may hold values from 0.5 to 1.5
- gate_weight: bfloat16 [16, 2048, 1024], P('expert', 'shard'), may hold values from -0.125 to 0.125
- up_weight: bfloat16 [16, 2048, 1024], P('expert', 'shard'), may hold values from -0.125 to 0.125
- down_weight: bfloat16 [16, 1024, 2048], P('expert', 'shard'), may hold values from -3 to 3
- permutation: int32 [2, 4, 1024], P(None, 'shard'), may hold values from 0 to 1023, each once within a row
- lengths: int32 [2, 4, 3], P(None, 'shard'), may hold values from 1 to 682, 1024 in all within a row
- routes: int32 [2, 4096, 8], P(None, ('expert', 'shard')), may hold values from 0 to 15, all different within a row
Outputs:
- output: bfloat16 [2, 4096, 2048], P(None, ('expert', 'shard'))
- input_grad: bfloat16 [2, 4096, 2048], P(None, ('expert', 'shard'))
- qkv_grad: float32 [2048, 6144], P(('expert', 'shard'))
- out_grad: float32 [2048, 2048], P(('expert', 'shard'))
- router_grad: float32 [2048, 16], P(('expert', 'shard'))
- attn_gain_grad: float32 [2048], P(('expert', 'shard'))
- moe_gain_grad: float32 [2048], P(('expert', 'shard'))
- head_gain_grad: float32 [256], P(('expert', 'shard'))
- gate_grad: float32 [16, 2048, 1024], P('expert', 'shard')
- up_grad: float32 [16, 2048, 1024], P('expert', 'shard')
- down_grad: float32 [16, 1024, 2048], P('expert', 'shard')
The draws below stay inside these ranges and needn't reach their ends.
Inputs may be any that keep to these rules, and one draw needn't show every extreme that they name: `lengths`: each row sums to 1024; its largest entry is 682. `routes`: the 8 experts of a token differ.
All inputs are finite; a program needn't handle non-finite values.
Results may differ from the reference program's by a relative error of at most 0.03.
Values may be sent and summed in bfloat16 or wider, within the bound.
No kernel may reach another device: no remote copies, remote signals or barrier semaphores. Data moves between devices by JAX's collectives and lax.ppermute only.
A program may use at most 448 MiB of HBM per device.

```python
import math
import jax
import jax.numpy as jnp
import numpy as np
from jax import lax

D = 2048
HEADS = 16
HEAD = 128
FF = 1024
TOPK = 8
MICRO = 2
SEQS = 3
TOK_MB = 128
EXPERTS = 16
GROUPS = 4
GROUP = 1024
LONGEST = 682
TOKENS_MB = 4096
CAP = 64
N_EXPERT = 8
N_SHARD = 4
DEVICES = 32


def level_of(stream_key, shape, cuts, low, top_value):
    def one(axis_at, shards_of):
        draws = jax.random.uniform(jax.random.fold_in(jax.random.fold_in(stream_key, 6), axis_at), (shards_of,), jnp.float32, low / len(cuts), top_value / len(cuts))
        return jnp.repeat(jnp.exp(draws), shape[axis_at] // shards_of).reshape((-1,) + (1,) * (len(shape) - axis_at - 1))

    loudness = one(*cuts[0])
    for cut in cuts[1:]:
        loudness = loudness * one(*cut)
    return loudness


def choose_distinct(stream_key, rows, count, top, lift):
    order = jax.random.permutation(jax.random.fold_in(stream_key, 1), count)
    pull = order
    for power in range(3):
        pull = pull * pull // count
    pull = pull * lift // count
    lots = jax.random.randint(jax.random.fold_in(stream_key, 2), (rows, count), 0, 4096) + pull
    fixed_rows = jax.random.permutation(jax.random.fold_in(stream_key, 3), rows)[jnp.arange(count) % rows]
    lots = jnp.where(jnp.arange(rows)[:, None] == fixed_rows[None, :], 1 << 14, lots)
    merit = lots * count + jnp.arange(count)
    return lax.top_k(merit.astype(jnp.int32), top)[1].astype(jnp.int32)


def profile(amount, total, limit, slope):
    weights = [(1 << 20) // math.isqrt(grade ** slope) + 1 for grade in range(2, amount + 1)]
    surplus, given = total - limit - (amount - 1), [1] * (amount - 1)
    while surplus > 0:
        free = [i for i in range(amount - 1) if given[i] < limit]
        whole, left = sum([weights[i] for i in free]), surplus
        for i in free:
            extra = min(limit - given[i], max(1, left * weights[i] // whole), surplus)
            given[i] = given[i] + extra
            surplus = surplus - extra
    return np.array([limit] + given)


def uneven_parts(rng, amount, total, most, slope):
    if amount == 2:
        one = jax.random.randint(rng, (), max(1, total - most), min(most, total - 1) + 1)
        return jnp.stack([one, total - one])
    sizes = jnp.asarray(profile(amount, total, most, slope), jnp.int32)
    couples = (amount - 1) // 2
    giver, receiver = sizes[1:1 + 2 * couples:2], sizes[2:2 + 2 * couples:2]
    slack = jnp.minimum(giver - 1, most - receiver)
    moved = jax.random.randint(jax.random.fold_in(rng, 1), (couples,), 0, 1 << 20) % (slack + 1)
    sizes = sizes.at[1:1 + 2 * couples:2].set(giver - moved).at[2:2 + 2 * couples:2].set(receiver + moved)
    return sizes[jax.random.permutation(jax.random.fold_in(rng, 2), amount)]


def gaussian(key, shape, width, bound, split=(), kind=jnp.bfloat16):
    values = width * jax.random.normal(key, shape, jnp.float32)
    if split:
        values = values * level_of(key, shape, split, -0.22, 0.18)
    return jnp.clip(values, -bound, bound).astype(kind)


def setup_inputs(seed: int = 0) -> dict:
    streams_of = jax.random.split(jax.random.key(seed), 15)
    return {
        "tokens": gaussian(streams_of[0], (MICRO, TOKENS_MB, D), 1.0, 6.0, ((1, 32),)),
        "cotangent": gaussian(streams_of[1], (MICRO, TOKENS_MB, D), 1.0, 6.0, ((1, 32),)),
        "qkv_weight": gaussian(streams_of[2], (D, 3 * D), D ** -0.5, 0.125),
        "out_weight": gaussian(streams_of[3], (D, D), (max(1, 4 * D // LONGEST)) ** -0.5, 1.75),
        "router_weight": gaussian(streams_of[4], (D, EXPERTS), (4 * D) ** -0.5, 0.0625),
        "attn_gain": jnp.clip(1.0 + 0.1 * jax.random.normal(streams_of[5], (D,), jnp.float32), 0.5, 1.5),
        "moe_gain": jnp.clip(1.0 + 0.1 * jax.random.normal(streams_of[6], (D,), jnp.float32), 0.5, 1.5),
        "head_gains": jnp.clip(1.0 + 0.1 * jax.random.normal(streams_of[7], (2 * HEAD,), jnp.float32), 0.5, 1.5),
        "gate_weight": gaussian(streams_of[8], (EXPERTS, D, FF), D ** -0.5, 0.125, ((0, 8), (1, 4))),
        "up_weight": gaussian(streams_of[9], (EXPERTS, D, FF), D ** -0.5, 0.125, ((0, 8), (1, 4))),
        "down_weight": gaussian(streams_of[10], (EXPERTS, FF, D), (max(1, FF // 256)) ** -0.5, 3.0, ((0, 8), (1, 4))),
        "permutation": jax.vmap(lambda own: jax.random.permutation(own, GROUP))(jax.random.split(streams_of[11], MICRO * GROUPS)).reshape((MICRO, GROUPS, GROUP)).astype(jnp.int32),
        "lengths": jax.vmap(lambda own: uneven_parts(own, SEQS, GROUP, LONGEST, 2))(jax.random.split(streams_of[12], MICRO * GROUPS)).reshape((MICRO, GROUPS, SEQS)).astype(jnp.int32),
        "routes": choose_distinct(streams_of[13], MICRO * TOKENS_MB, EXPERTS, TOPK, 4096).reshape((MICRO, TOKENS_MB, TOPK)),
    }


EPS = 1e-06
ROPE_BASE = 10000.0
NEGATIVE = -1e+30
HIGHEST = lax.Precision.HIGHEST

@jax.custom_vjp
def low(v):
    return lax.optimization_barrier(v.astype(jnp.bfloat16)).astype(jnp.float32)

@jax.custom_vjp
def low_back(v):
    return v

def low_keep(v):
    return (low(v), None)

def low_pass(kept, grad):
    return (grad,)

def back_keep(v):
    return (v, None)

def back_low(kept, grad):
    return (low(grad),)
low.defvjp(low_keep, low_pass)
low_back.defvjp(back_keep, back_low)

def rms_scale(values, gain_vec):
    return values * lax.rsqrt(lax.optimization_barrier(jnp.mean(values * values, axis=-1, keepdims=True)) + EPS) * gain_vec

def rotate(values, cosine, sine):
    half_size = values.shape[-1] // 2
    lower_half = values[..., :half_size]
    upper_half = values[..., half_size:]
    return jnp.concatenate([lower_half * cosine - upper_half * sine, upper_half * cosine + lower_half * sine], axis=-1)

def places(perm_row, length_row):
    seq_ends = jnp.cumsum(length_row)
    seg_ids = lax.optimization_barrier(jnp.sum((perm_row[:, None] >= seq_ends[None, :]).astype(jnp.int32), axis=1))
    starts = seq_ends - length_row
    pick_mask = seg_ids[:, None] == jnp.arange(length_row.shape[0], dtype=jnp.int32)[None, :]
    seq_begin = lax.optimization_barrier(jnp.sum(jnp.where(pick_mask, starts[None, :], 0), axis=1))
    return (seg_ids, perm_row - seq_begin)

def angles(positions):
    half_size = HEAD // 2
    frequency = jnp.power(ROPE_BASE, -2.0 * jnp.arange(half_size, dtype=jnp.float32) / HEAD)
    turned = positions.astype(jnp.float32)[:, None] * frequency[None, :]
    return (jnp.cos(turned)[:, None, :], jnp.sin(turned)[:, None, :])

def head_prep(qkv_out, head_gains, cosine, sine):
    model_width = qkv_out.shape[1] // 3
    row_count = qkv_out.shape[0]
    query_rows = qkv_out[:, :model_width].reshape(row_count, model_width // HEAD, HEAD)
    key_rows = qkv_out[:, model_width:2 * model_width].reshape(row_count, model_width // HEAD, HEAD)
    value_rows = qkv_out[:, 2 * model_width:]
    query_rows = rotate(rms_scale(query_rows, head_gains[:HEAD]), cosine, sine)
    key_rows = rotate(rms_scale(key_rows, head_gains[HEAD:]), cosine, sine)
    return (query_rows.reshape(row_count, model_width), key_rows.reshape(row_count, model_width), value_rows)

def to_groups(array):
    tail_dims = array.shape[1:]
    return jnp.swapaxes(array.reshape((N_EXPERT, N_SHARD, TOK_MB) + tail_dims), 0, 1).reshape((N_SHARD, N_EXPERT * TOK_MB) + tail_dims)

def from_groups(array):
    tail_dims = array.shape[2:]
    return jnp.swapaxes(array.reshape((N_SHARD, N_EXPERT, TOK_MB) + tail_dims), 0, 1).reshape((N_SHARD * N_EXPERT * TOK_MB,) + tail_dims)

def attend(query_g, key_g, value_g, seg_g):
    raw_scores = jnp.einsum('qhd,khd->hqk', query_g, key_g, precision=HIGHEST) * HEAD ** (-0.5)
    raw_scores = low_back(raw_scores)
    same_seq = (seg_g[:, None] == seg_g[None, :])[None]
    masked = jnp.where(same_seq, raw_scores, NEGATIVE)
    exp_terms = jnp.exp(masked - lax.optimization_barrier(jnp.max(masked, axis=-1, keepdims=True)))
    probs = exp_terms / lax.optimization_barrier(jnp.sum(exp_terms, axis=-1, keepdims=True))
    probs = low(probs)
    return jnp.einsum('hqk,khd->qhd', probs, value_g, precision=HIGHEST)

def layer(inputs, qkv_weight, out_weight, router_weight, attn_gain, moe_gain, head_gains, gate_weight, up_weight, down_weight, perm_part, length_part, route_part):
    seg_ids, positions = jax.vmap(places)(perm_part, length_part)
    cosine, sine = angles(from_groups(positions))
    normed_attn = low(rms_scale(inputs, attn_gain))
    qkv_out = low_back(jnp.dot(normed_attn, qkv_weight, precision=HIGHEST))
    query_rows, key_rows, value_rows = head_prep(qkv_out, head_gains, cosine, sine)
    query_g = to_groups(low(query_rows).reshape(-1, HEADS, HEAD))
    key_g = to_groups(low(key_rows).reshape(-1, HEADS, HEAD))
    value_g = to_groups(low(value_rows).reshape(-1, HEADS, HEAD))
    attended = lax.map(lambda group_in: jax.checkpoint(attend)(*group_in), (query_g, key_g, value_g, seg_ids))
    attended = low_back(low(from_groups(attended).reshape(-1, D)))
    mixed = inputs + low_back(jnp.dot(attended, out_weight, precision=HIGHEST))
    normed_moe = low(rms_scale(mixed, moe_gain))
    logits = low_back(jnp.dot(normed_moe, router_weight, precision=HIGHEST))
    exp_logits = jnp.exp(logits - lax.optimization_barrier(jnp.max(logits, axis=-1, keepdims=True)))
    router = exp_logits / lax.optimization_barrier(jnp.sum(exp_logits, axis=-1, keepdims=True))
    expert_ids = jnp.arange(EXPERTS, dtype=jnp.int32)
    dev_routes = route_part.reshape(DEVICES, TOK_MB * TOPK)
    hot_int = (dev_routes[:, :, None] == expert_ids[None, None, :]).astype(jnp.int32)
    earlier = jnp.cumsum(hot_int, axis=1) - hot_int
    slot_ids = lax.optimization_barrier(jnp.sum(earlier * hot_int, axis=-1)).reshape(TOKENS_MB, TOPK)
    keep_pair = slot_ids < CAP
    token_dev = jnp.arange(TOKENS_MB, dtype=jnp.int32) // TOK_MB
    row_index = token_dev[:, None] * CAP + slot_ids

    def expert_step(carry, item):
        expert_id, gate_w, up_w, down_w = item
        hit_pair = (route_part == expert_id) & keep_pair
        has_pair = jnp.any(hit_pair, axis=1)
        row_pick = lax.optimization_barrier(jnp.sum(jnp.where(hit_pair, row_index, 0), axis=1))
        dest_row = jnp.where(has_pair, row_pick, DEVICES * CAP)
        buffer = jnp.zeros((DEVICES * CAP + 1, D), jnp.float32).at[dest_row].add(normed_moe)[:DEVICES * CAP]
        buffer = low_back(buffer)
        gate_act = low_back(jnp.dot(buffer, gate_w, precision=HIGHEST))
        up_act = low_back(jnp.dot(buffer, up_w, precision=HIGHEST))
        hidden_act = low(jax.nn.silu(gate_act) * up_act)
        result = low_back(low(jnp.dot(hidden_act, down_w, precision=HIGHEST)))
        gate_col = lax.optimization_barrier(jnp.sum(jnp.where(expert_ids[None, :] == expert_id, router, 0.0), axis=1))
        fetched = result[jnp.minimum(row_pick, DEVICES * CAP - 1)]
        return (carry + jnp.where(has_pair[:, None], gate_col[:, None] * fetched, 0.0), None)
    moe_part, _ = lax.scan(jax.checkpoint(expert_step), jnp.zeros_like(inputs), (expert_ids, gate_weight, up_weight, down_weight))
    return mixed + moe_part

def reference(tokens, cotangent, qkv_weight, out_weight, router_weight, attn_gain, moe_gain, head_gains, gate_weight, up_weight, down_weight, permutation, lengths, routes):
    params = jax.tree.map(lambda array: array.astype(jnp.float32), (qkv_weight, out_weight, router_weight, attn_gain, moe_gain, head_gains, gate_weight, up_weight, down_weight))
    outputs = []
    input_grads = []
    totals = None
    for micro_step in range(MICRO):

        def forward(inputs, *weights):
            return layer(inputs, *weights, permutation[micro_step], lengths[micro_step], routes[micro_step])
        result, pull_back = jax.vjp(forward, tokens[micro_step].astype(jnp.float32), *params)
        gradients = pull_back(cotangent[micro_step].astype(jnp.float32))
        outputs.append(result.astype(jnp.bfloat16))
        input_grads.append(gradients[0].astype(jnp.bfloat16))
        if totals is None:
            totals = gradients[1:]
        else:
            totals = jax.tree.map(jnp.add, totals, gradients[1:])
    return (jnp.stack(outputs), jnp.stack(input_grads), totals[0], totals[1], totals[2], totals[3], totals[4], totals[5], totals[6], totals[7], totals[8])
```

```python
import jax
import jax.numpy as jnp
from jax import lax
from jax.sharding import PartitionSpec as P

HEAD = 128
EPS = 1e-06
ROPE_BASE = 10000.0
NEGATIVE = -1e30
LOW = jnp.bfloat16
F32 = jnp.float32


def rms_scale(values, gain_vec):
    return values * lax.rsqrt(jnp.mean(values * values, axis=-1, keepdims=True) + EPS) * gain_vec


def rotate(values, cosine, sine):
    half_size = values.shape[-1] // 2
    lower_half = values[..., :half_size]
    upper_half = values[..., half_size:]
    return jnp.concatenate(
        [lower_half * cosine - upper_half * sine, upper_half * cosine + lower_half * sine], axis=-1
    )


def places(perm_row, length_row):
    seq_ends = jnp.cumsum(length_row)
    seg_ids = jnp.sum((perm_row[:, None] >= seq_ends[None, :]).astype(jnp.int32), axis=1)
    starts = seq_ends - length_row
    pick_mask = seg_ids[:, None] == jnp.arange(length_row.shape[0], dtype=jnp.int32)[None, :]
    seq_begin = jnp.sum(jnp.where(pick_mask, starts[None, :], 0), axis=1)
    return (seg_ids, perm_row - seq_begin)


def angles(positions):
    half_size = HEAD // 2
    frequency = jnp.power(ROPE_BASE, -2.0 * jnp.arange(half_size, dtype=F32) / HEAD)
    turned = positions.astype(F32)[:, None] * frequency[None, :]
    return (jnp.cos(turned)[:, None, :], jnp.sin(turned)[:, None, :])


def head_prep(qkv_out, head_gains, cosine, sine):
    width = qkv_out.shape[1] // 3
    row_count = qkv_out.shape[0]
    query_rows = qkv_out[:, :width].reshape(row_count, width // HEAD, HEAD)
    key_rows = qkv_out[:, width : 2 * width].reshape(row_count, width // HEAD, HEAD)
    value_rows = qkv_out[:, 2 * width :].reshape(row_count, width // HEAD, HEAD)
    query_rows = rotate(rms_scale(query_rows, head_gains[:HEAD]), cosine, sine)
    key_rows = rotate(rms_scale(key_rows, head_gains[HEAD:]), cosine, sine)
    return (query_rows, key_rows, value_rows)


def swiglu(gate_in, up_in):
    return jax.nn.silu(gate_in) * up_in


def hop(value, axis, step):
    size = lax.axis_size(axis)
    return lax.ppermute(value, axis, [(i, i ^ step) for i in range(size)])


def gather_blocks(value, axis):
    size = lax.axis_size(axis)
    blocks = [None] * size
    blocks[0] = value
    for k in range(size - 2, 0, -2):
        blocks[k] = hop(value, axis, k)
    for k in [0] + list(range(size - 2, 0, -2)):
        blocks[k + 1] = hop(blocks[k], axis, 1)
    return blocks


def scatter_blocks(blocks, axis):
    size = len(blocks)
    half = {}
    for k in list(range(size - 2, 0, -2)) + [0]:
        half[k] = blocks[k].astype(F32) + hop(blocks[k + 1], axis, 1).astype(F32)
    total = half[0]
    for k in range(size - 2, 0, -2):
        total = total + hop(half[k].astype(LOW), axis, k).astype(F32)
    return total


def place_blocks(blocks, own, dim):
    size = blocks[0].shape[dim]
    shape = list(blocks[0].shape)
    shape[dim] = size * len(blocks)
    whole = jnp.zeros(shape, blocks[0].dtype)
    for k, block in enumerate(blocks):
        whole = lax.dynamic_update_slice_in_dim(whole, block, (own ^ k) * size, dim)
    return whole


def take_blocks(whole, own, count, dim):
    size = whole.shape[dim] // count
    return [lax.dynamic_slice_in_dim(whole, (own ^ k) * size, size, dim) for k in range(count)]


def swap(value, axis):
    return lax.all_to_all(value, axis, split_axis=0, concat_axis=0, tiled=True)


def dot(a, b):
    return jnp.dot(a, b, preferred_element_type=F32)


def ein(spec, a, b):
    return jnp.einsum(spec, a, b, preferred_element_type=F32)


def local(
    tokens,
    cotangent,
    qkv_weight,
    out_weight,
    router_weight,
    attn_gain,
    moe_gain,
    head_gains,
    gate_weight,
    up_weight,
    down_weight,
    permutation,
    lengths,
    routes,
):
    micro_count, rows, width = tokens.shape
    score_scale = HEAD ** (-0.5)
    n = lax.axis_size("expert")
    m = lax.axis_size("shard")
    own = lax.axis_index("expert")
    own_shard = lax.axis_index("shard")
    local_count = gate_weight.shape[0]
    expert_count = local_count * n
    top_count = routes.shape[2]
    capacity = rows * top_count // expert_count
    group = n * rows
    part = width // n
    heads = part // HEAD
    ff = gate_weight.shape[2]

    qkv_own = lax.dynamic_slice_in_dim(
        qkv_weight.reshape(width, 3, width), own * part, part, 2
    ).reshape(width, 3 * part)

    inputs = [tokens[i].astype(F32) for i in range(micro_count)]
    normed_attn = [rms_scale(x, attn_gain).astype(LOW) for x in inputs]
    normed_all = [place_blocks(gather_blocks(v, "expert"), own, 0) for v in normed_attn]

    gate_parts = gather_blocks(gate_weight, "shard")
    up_parts = gather_blocks(up_weight, "shard")
    down_parts = gather_blocks(down_weight, "shard")
    full_gate = place_blocks(gate_parts, own_shard, 1)
    full_up = place_blocks(up_parts, own_shard, 1)
    full_down = place_blocks(down_parts, own_shard, 1)

    grad_all = lax.all_gather(cotangent, "expert", axis=1, tiled=True)
    routes_all = lax.all_gather(routes, "expert", axis=0)

    own_experts = own * local_count + jnp.arange(local_count, dtype=jnp.int32)
    slot_iota = jnp.arange(capacity, dtype=jnp.int32)

    saved = []
    for i in range(micro_count):
        seg, pos = places(permutation[i, 0], lengths[i, 0])
        cosine, sine = angles(pos)
        qkv_out = dot(normed_all[i], qkv_own)
        query, key, value = head_prep(qkv_out, head_gains, cosine, sine)
        query, key, value = query.astype(LOW), key.astype(LOW), value.astype(LOW)
        same_seq = (seg[:, None] == seg[None, :])[None]
        raw = ein("qhd,khd->hqk", query, key) * score_scale
        scores = jnp.where(same_seq, raw, NEGATIVE)
        top = jnp.max(scores, axis=-1, keepdims=True)
        terms = jnp.exp(scores - top)
        total = jnp.sum(terms, axis=-1, keepdims=True)
        probs = terms / total
        log_total = top + jnp.log(total)
        attended = ein("hqk,khd->qhd", probs.astype(LOW), value).astype(LOW)
        attended = swap(attended.reshape(n, rows, part), "expert")
        attended = jnp.swapaxes(attended, 0, 1).reshape(rows, width)
        mixed = inputs[i] + dot(attended, out_weight)
        normed_moe = rms_scale(mixed, moe_gain).astype(LOW)
        saved.append(
            dict(
                cosine=cosine, sine=sine, qkv_out=qkv_out, query=query, key=key, value=value,
                same_seq=same_seq, log_total=log_total, attended=attended, mixed=mixed,
                normed_moe=normed_moe,
            )
        )

    experts = []
    for i in range(micro_count):
        normed_moe = saved[i]["normed_moe"]
        moe_all = place_blocks(gather_blocks(normed_moe, "expert"), own, 0)
        logits = dot(moe_all, router_weight)
        exp_logits = jnp.exp(logits - jnp.max(logits, axis=-1, keepdims=True))
        router = exp_logits / jnp.sum(exp_logits, axis=-1, keepdims=True)
        hit = jnp.any(
            routes_all[:, i][:, None, :, :] == own_experts[None, :, None, None], axis=-1
        )
        hot = hit.astype(jnp.int32)
        slot = jnp.cumsum(hot, axis=-1) - hot
        pick = hit[:, :, None, :] & (slot[:, :, None, :] == slot_iota[None, None, :, None])
        pick = jnp.swapaxes(pick, 0, 1)
        pick_low = pick.astype(LOW)
        own_router = lax.dynamic_slice_in_dim(router, own * local_count, local_count, 1)
        own_router = own_router.reshape(n, rows, local_count).transpose(2, 0, 1)
        gate_col = jnp.sum(jnp.where(pick, own_router[:, :, None, :], 0.0), axis=-1)
        blocks_in = moe_all.reshape(n, rows, width)
        blocks_grad = grad_all[i].reshape(n, rows, width)
        buffer = ein("ebct,btd->ebcd", pick_low, blocks_in).astype(LOW)
        buffer = buffer.reshape(local_count, n * capacity, width)
        grad_rows = ein("ebct,btd->ebcd", pick_low, blocks_grad)
        d_result = (gate_col[..., None] * grad_rows).astype(LOW)
        d_result = d_result.reshape(local_count, n * capacity, width)
        gate_act = ein("erd,edf->erf", buffer, full_gate)
        up_act = ein("erd,edf->erf", buffer, full_up)
        hidden, pull = jax.vjp(swiglu, gate_act, up_act)
        hidden = hidden.astype(LOW)
        result = ein("erf,efd->erd", hidden, full_down).astype(LOW)
        result_b = result.reshape(local_count, n, capacity, width)
        d_gate = jnp.sum(result_b.astype(F32) * grad_rows, axis=-1)
        d_gate_tok = jnp.sum(jnp.where(pick, d_gate[..., None], 0.0), axis=2)
        d_gate_tok = jnp.swapaxes(d_gate_tok, 0, 1)
        weigh = (jnp.where(pick, gate_col[..., None], 0.0)).astype(LOW)
        moe_sum = ein("ebct,ebcd->btd", weigh, result_b).astype(LOW)
        d_hidden = ein("erd,efd->erf", d_result, full_down)
        d_gate_act, d_up_act = pull(d_hidden)
        d_gate_act, d_up_act = d_gate_act.astype(LOW), d_up_act.astype(LOW)
        d_buffer = (
            ein("erf,edf->erd", d_gate_act, full_gate) + ein("erf,edf->erd", d_up_act, full_up)
        ).astype(LOW)
        d_sum = ein(
            "ebct,ebcd->btd", pick_low, d_buffer.reshape(local_count, n, capacity, width)
        ).astype(LOW)
        d_gates = swap(d_gate_tok, "expert")
        d_router = d_gates.reshape(expert_count, rows).T
        d_normed = scatter_blocks(take_blocks(d_sum.reshape(group, width), own, n, 0), "expert")
        moe_part = scatter_blocks(
            take_blocks(moe_sum.reshape(group, width), own, n, 0), "expert"
        )
        router_own = lax.dynamic_slice_in_dim(router, own * rows, rows, 0)
        experts.append(
            dict(
                buffer=buffer, hidden=hidden, d_result=d_result, d_gate_act=d_gate_act,
                d_up_act=d_up_act, d_router=d_router, d_normed=d_normed, moe_part=moe_part,
                router=router_own,
            )
        )

    both = {
        name: jnp.concatenate([x[name] for x in experts], axis=1)
        for name in ("buffer", "hidden", "d_result", "d_gate_act", "d_up_act")
    }
    gate_term = ein("erd,erf->edf", both["buffer"], both["d_gate_act"]).astype(LOW)
    up_term = ein("erd,erf->edf", both["buffer"], both["d_up_act"]).astype(LOW)
    down_term = ein("erf,erd->efd", both["hidden"], both["d_result"]).astype(LOW)
    gate_grad, up_grad, down_grad = (
        scatter_blocks(take_blocks(term, own_shard, m, 1), "shard")
        for term in (gate_term, up_term, down_term)
    )

    outputs = [
        (saved[i]["mixed"] + experts[i]["moe_part"]).astype(LOW) for i in range(micro_count)
    ]

    router_term = 0.0
    moe_gain_term = 0.0
    attn_gain_term = 0.0
    head_term = 0.0
    d_mixed_all, d_attn_all, d_qkv_all = [], [], []
    for i in range(micro_count):
        state, moe = saved[i], experts[i]
        grad_out = cotangent[i].astype(F32)
        router = moe["router"]
        d_router = moe["d_router"]
        d_logits = (
            router * (d_router - jnp.sum(router * d_router, axis=-1, keepdims=True))
        ).astype(LOW)
        d_normed = moe["d_normed"] + dot(d_logits, router_weight.T)
        router_term = router_term + dot(state["normed_moe"].T, d_logits)
        _, norm_pull = jax.vjp(rms_scale, state["mixed"], moe_gain)
        d_mixed_norm, gain_term = norm_pull(d_normed)
        moe_gain_term = moe_gain_term + gain_term
        d_mixed = grad_out + d_mixed_norm
        d_attn = d_mixed.astype(LOW)
        d_mixed_all.append(d_mixed)
        d_attn_all.append(d_attn)
        d_attended = dot(d_attn, out_weight.T).astype(LOW)
        d_attended = swap(jnp.swapaxes(d_attended.reshape(rows, n, part), 0, 1), "expert")
        d_attended = d_attended.reshape(group, heads, HEAD)
        query, key, value = state["query"], state["key"], state["value"]
        raw = ein("qhd,khd->hqk", query, key) * score_scale
        probs = jnp.exp(jnp.where(state["same_seq"], raw, NEGATIVE) - state["log_total"])
        d_probs = ein("qhd,khd->hqk", d_attended, value)
        delta = jnp.sum(probs * d_probs, axis=-1, keepdims=True)
        d_scores = (probs * (d_probs - delta)).astype(LOW)
        d_query = ein("hqk,khd->qhd", d_scores, key) * score_scale
        d_key = ein("hqk,qhd->khd", d_scores, query) * score_scale
        d_value = ein("hqk,qhd->khd", probs.astype(LOW), d_attended)
        _, head_pull = jax.vjp(
            lambda qkv_in, gains_in: head_prep(qkv_in, gains_in, state["cosine"], state["sine"]),
            state["qkv_out"],
            head_gains,
        )
        d_qkv, term = head_pull((d_query, d_key, d_value))
        head_term = head_term + term
        d_qkv = d_qkv.astype(LOW)
        d_qkv_all.append(d_qkv)
        d_qkv_rows = swap(d_qkv.reshape(n, rows, 3 * part), "expert")
        d_qkv_rows = d_qkv_rows.reshape(n, rows, 3, part).transpose(1, 2, 0, 3)
        d_normed_attn = dot(d_qkv_rows.reshape(rows, 3 * width), qkv_weight.T)
        _, attn_pull = jax.vjp(rms_scale, inputs[i], attn_gain)
        d_inputs_norm, term = attn_pull(d_normed_attn)
        attn_gain_term = attn_gain_term + term
        state["input_grad"] = (d_mixed + d_inputs_norm).astype(LOW)

    out_term = dot(
        jnp.concatenate([x["attended"] for x in saved], axis=0).T,
        jnp.concatenate(d_attn_all, axis=0),
    ).astype(LOW)
    out_grad = lax.psum_scatter(
        out_term, ("expert", "shard"), scatter_dimension=0, tiled=True
    ).astype(F32)

    qkv_term = dot(
        jnp.concatenate(normed_all, axis=0).T, jnp.concatenate(d_qkv_all, axis=0)
    ).astype(LOW)
    piece = width // (n * m)
    qkv_term = jnp.swapaxes(qkv_term.reshape(n, m, piece * 3 * part), 0, 1)
    qkv_sum = scatter_blocks(take_blocks(qkv_term, own_shard, m, 0), "shard").astype(LOW)
    qkv_rows = swap(qkv_sum.reshape(n, piece, 3 * part), "expert")
    qkv_grad = (
        qkv_rows.reshape(n, piece, 3, part).transpose(1, 2, 0, 3).reshape(piece, 3 * width)
    ).astype(F32)

    world = n * m
    head_piece = 2 * HEAD // world
    small = jnp.concatenate(
        [
            router_term.reshape(world, piece * expert_count),
            attn_gain_term.reshape(world, piece),
            moe_gain_term.reshape(world, piece),
            head_term.reshape(world, head_piece),
        ],
        axis=1,
    )
    used = small.shape[1]
    padded = -(-used // 1024) * 1024
    small = jnp.pad(small, ((0, 0), (0, padded - used))).reshape(world, padded // 128, 128)
    small = jnp.sum(swap(small, ("expert", "shard")), axis=0).reshape(padded)
    a = piece * expert_count
    return (
        jnp.stack(outputs),
        jnp.stack([x["input_grad"] for x in saved]),
        qkv_grad,
        out_grad,
        small[:a].reshape(piece, expert_count),
        small[a : a + piece],
        small[a + piece : a + 2 * piece],
        small[a + 2 * piece : a + 2 * piece + head_piece],
        gate_grad,
        up_grad,
        down_grad,
    )


def solution(mesh):
    return jax.shard_map(
        local,
        mesh=mesh,
        in_specs=(
            P(None, ("expert", "shard"), None),
            P(None, ("expert", "shard"), None),
            P(),
            P(),
            P(),
            P(),
            P(),
            P(),
            P("expert", "shard", None),
            P("expert", "shard", None),
            P("expert", "shard", None),
            P(None, "shard", None),
            P(None, "shard", None),
            P(None, ("expert", "shard"), None),
        ),
        out_specs=(
            P(None, ("expert", "shard"), None),
            P(None, ("expert", "shard"), None),
            P(("expert", "shard"), None),
            P(("expert", "shard"), None),
            P(("expert", "shard"), None),
            P(("expert", "shard")),
            P(("expert", "shard")),
            P(("expert", "shard")),
            P("expert", "shard", None),
            P("expert", "shard", None),
            P("expert", "shard", None),
        ),
        check_vma=False,
    )
```

```python
import functools

import jax
import jax.numpy as jnp
from jax import lax
from jax.experimental import pallas as pl
from jax.experimental.pallas import tpu as pltpu
from jax.sharding import PartitionSpec as P

HEAD = 128
EPS = 1e-06
ROPE_BASE = 10000.0
NEGATIVE = -1e30
LOW = jnp.bfloat16
F32 = jnp.float32


def rms_scale(values, gain_vec):
    return values * lax.rsqrt(jnp.mean(values * values, axis=-1, keepdims=True) + EPS) * gain_vec


def places(perm_row, length_row):
    seq_ends = jnp.cumsum(length_row)
    seg_ids = jnp.sum((perm_row[:, None] >= seq_ends[None, :]).astype(jnp.int32), axis=1)
    starts = seq_ends - length_row
    pick_mask = seg_ids[:, None] == jnp.arange(length_row.shape[0], dtype=jnp.int32)[None, :]
    seq_begin = jnp.sum(jnp.where(pick_mask, starts[None, :], 0), axis=1)
    return (seg_ids, perm_row - seq_begin)


def angles(positions):
    half_size = HEAD // 2
    frequency = jnp.power(ROPE_BASE, -2.0 * jnp.arange(half_size, dtype=F32) / HEAD)
    turned = positions.astype(F32)[..., None] * frequency
    cosine, sine = jnp.cos(turned), jnp.sin(turned)
    return (
        jnp.concatenate([cosine, cosine], axis=-1),
        jnp.concatenate([-sine, sine], axis=-1),
    )


def hop(value, axis, step):
    size = lax.axis_size(axis)
    return lax.ppermute(value, axis, [(i, i ^ step) for i in range(size)])


def gather_first(value, axis):
    size = lax.axis_size(axis)
    blocks = [None] * size
    blocks[0] = value
    for k in range(2, size, 2):
        blocks[k] = hop(value, axis, k)
    return blocks


def gather_second(blocks, axis):
    blocks = list(blocks)
    for k in range(0, len(blocks), 2):
        blocks[k + 1] = hop(blocks[k], axis, 1)
    return blocks


def gather_blocks(value, axis):
    return gather_second(gather_first(value, axis), axis)


def scatter_first(blocks, axis):
    return {
        k: (blocks[k].astype(F32) + hop(blocks[k + 1], axis, 1).astype(F32)).astype(LOW)
        for k in range(len(blocks) - 2, -1, -2)
    }


def scatter_second(half, axis):
    total = half[0].astype(F32)
    for k in sorted(half):
        if k:
            total = total + hop(half[k], axis, k).astype(F32)
    return total


def scatter_blocks(blocks, axis):
    return scatter_second(scatter_first(blocks, axis), axis)


def place_blocks(blocks, own, dim):
    size = blocks[0].shape[dim]
    shape = list(blocks[0].shape)
    shape[dim] = size * len(blocks)
    whole = jnp.zeros(shape, blocks[0].dtype)
    for k, block in enumerate(blocks):
        whole = lax.dynamic_update_slice_in_dim(whole, block, (own ^ k) * size, dim)
    return whole


def take_blocks(whole, own, count, dim):
    size = whole.shape[dim] // count
    return [lax.dynamic_slice_in_dim(whole, (own ^ k) * size, size, dim) for k in range(count)]


def swap(value, axis):
    return lax.all_to_all(value, axis, split_axis=0, concat_axis=0, tiled=True)


def dot(a, b):
    return jnp.dot(a, b, preferred_element_type=F32)


def ein(spec, a, b):
    return jnp.einsum(spec, a, b, preferred_element_type=F32)


def tie(value, *others):
    return lax.optimization_barrier((value, others))[0]


def mm(a, b, dims=((1,), (0,))):
    return lax.dot_general(a, b, (dims, ((), ())), preferred_element_type=F32)


def mm_nt(a, b):
    return mm(a, b, ((1,), (1,)))


def expert_kernel(n, tile, shared, own_ref, *refs):
    xs, cs = refs[:n], refs[n : 2 * n]
    pick_ref, turned_ref, router_ref, gate_ref, up_ref, down_ref = refs[2 * n : 2 * n + 6]
    outs = refs[2 * n + 6 + shared :]
    moe, dsum = outs[:n], outs[n : 2 * n]
    buffer_ref, d_result_ref, hidden_ref, dg_ref, du_ref, d_gate_ref = outs[2 * n : 2 * n + 6]
    acc_res, acc_db, grad_rows, gate_cols = outs[2 * n + 6 :]
    own = own_ref[0]
    expert, step, steps = pl.program_id(0), pl.program_id(1), pl.num_programs(1)
    cap = pick_ref.shape[3]
    index = own * pl.num_programs(0) + expert

    @pl.when(step == 0)
    def _():
        for k in range(n):
            span = pl.ds(k * cap, cap)
            block = xs[k][...]
            pick = pick_ref[0, 0, own ^ k]
            buffer_ref[0, span, :] = mm(pick, block).astype(LOW)
            logits = mm_nt(router_ref[...], block)
            terms = jnp.exp(logits - jnp.max(logits, axis=0, keepdims=True))
            router = terms / jnp.sum(terms, axis=0, keepdims=True)
            lines = lax.broadcasted_iota(jnp.int32, router.shape, 0)
            row = jnp.sum(jnp.where(lines == index, router, 0.0), axis=0, keepdims=True)
            col = jnp.sum(pick.astype(F32) * row, axis=1, keepdims=True)
            grads = mm(pick, cs[k][...])
            grad_rows[span, :] = grads.astype(LOW)
            d_result_ref[0, span, :] = (col * grads).astype(LOW)
            gate_cols[span, :] = jnp.broadcast_to(col, (cap, gate_cols.shape[1]))

    slots = n * cap
    for r in range(0, slots, tile):
        span = pl.ds(r, tile)
        rows_in = buffer_ref[0, span, :]
        gate_act = mm(rows_in, gate_ref[0])
        up_act = mm(rows_in, up_ref[0])
        d_hidden = mm_nt(d_result_ref[0, span, :], down_ref[0])
        sig = 1.0 / (1.0 + jnp.exp(-gate_act))
        silu = gate_act * sig
        hidden = (silu * up_act).astype(LOW)
        dg = (d_hidden * up_act * (sig * (1.0 + gate_act * (1.0 - sig)))).astype(LOW)
        du = (d_hidden * silu).astype(LOW)
        hidden_ref[0, span, :] = hidden
        dg_ref[0, span, :] = dg
        du_ref[0, span, :] = du

        @pl.when(step == 0)
        def _():
            acc_res[span, :] = mm(hidden_ref[0, span, :], down_ref[0])
            acc_db[span, :] = mm_nt(dg_ref[0, span, :], gate_ref[0]) + mm_nt(
                du_ref[0, span, :], up_ref[0]
            )

        @pl.when(step > 0)
        def _():
            acc_res[span, :] += mm(hidden_ref[0, span, :], down_ref[0])
            acc_db[span, :] += mm_nt(dg_ref[0, span, :], gate_ref[0]) + mm_nt(
                du_ref[0, span, :], up_ref[0]
            )

    @pl.when(step == steps - 1)
    def _():
        lines = lax.broadcasted_iota(jnp.int32, d_gate_ref.shape[1:], 0)
        d_gate = jnp.zeros(d_gate_ref.shape[1:], F32)
        for k in range(n):
            span = pl.ds(k * cap, cap)
            pick = pick_ref[0, 0, own ^ k]
            turned = turned_ref[0, 0, own ^ k]
            result = acc_res[span, :].astype(LOW).astype(F32)
            col = jnp.sum(result * grad_rows[span, :].astype(F32), axis=1, keepdims=True)
            row = jnp.sum(pick.astype(F32) * col, axis=0, keepdims=True)
            d_gate = jnp.where(lines == (own ^ k), row, d_gate)
            scaled = (gate_cols[span, :1] * result).astype(LOW)
            part = mm(turned, scaled)
            d_part = mm(turned, acc_db[span, :].astype(LOW))

            @pl.when(expert == 0)
            def _():
                moe[k][...] = part.astype(LOW)
                dsum[k][...] = d_part.astype(LOW)

            @pl.when(expert > 0)
            def _():
                moe[k][...] = (moe[k][...].astype(F32) + part).astype(LOW)
                dsum[k][...] = (dsum[k][...].astype(F32) + d_part).astype(LOW)

        d_gate_ref[0] = d_gate


def expert_layer(own, blocks, grads, pick, turned, router_turned, gate, up, down, at, micro, kept, tile=512):
    n = len(blocks)
    rows, width = blocks[0].shape
    count, _, ff = gate.shape
    cap = pick.shape[3]
    slots = n * cap
    split = 2 if n <= 8 else 4
    ft = ff // split
    one = dict(pipeline_mode=pl.Buffered(1))
    some = one if n > 8 else {}
    block = pl.BlockSpec((rows, width), lambda e, f, o: (0, 0), **one)
    row_block = pl.BlockSpec((1, slots, width), lambda e, f, o: (e, at, 0), **some)
    ff_block = pl.BlockSpec((1, slots, ft), lambda e, f, o: (e, at, f))
    tokens_shape = jax.ShapeDtypeStruct((rows, width), LOW)
    rows_shape = jax.ShapeDtypeStruct((count, micro * slots, width), LOW)
    ff_shape = jax.ShapeDtypeStruct((count, micro * slots, ff), LOW)
    kept = [] if kept is None else list(kept)
    before = 1 + 2 * n + 6
    outs = pl.pallas_call(
        functools.partial(expert_kernel, n, tile, len(kept)),
        out_shape=[tokens_shape] * (2 * n)
        + [rows_shape, rows_shape, ff_shape, ff_shape, ff_shape]
        + [jax.ShapeDtypeStruct((count, n, rows), F32)],
        grid_spec=pltpu.PrefetchScalarGridSpec(
            num_scalar_prefetch=1,
            grid=(count, split),
            in_specs=[block] * (2 * n)
            + [
                pl.BlockSpec((1, 1, n, cap, rows), lambda e, f, o: (e, at, 0, 0, 0), **some),
                pl.BlockSpec((1, 1, n, rows, cap), lambda e, f, o: (e, at, 0, 0, 0), **some),
                pl.BlockSpec(router_turned.shape, lambda e, f, o: (0, 0)),
                pl.BlockSpec((1, width, ft), lambda e, f, o: (e, 0, f)),
                pl.BlockSpec((1, width, ft), lambda e, f, o: (e, 0, f)),
                pl.BlockSpec((1, ft, width), lambda e, f, o: (e, f, 0)),
            ]
            + [pl.BlockSpec(memory_space=pl.ANY)] * len(kept),
            out_specs=[block] * (2 * n)
            + [row_block, row_block, ff_block, ff_block, ff_block]
            + [pl.BlockSpec((1, n, rows), lambda e, f, o: (e, 0, 0))],
            scratch_shapes=[
                pltpu.VMEM((slots, width), F32),
                pltpu.VMEM((slots, width), F32),
                pltpu.VMEM((slots, width), LOW),
                pltpu.VMEM((slots, 128), F32),
            ],
        ),
        input_output_aliases={before + i: 2 * n + i for i in range(len(kept))},
        compiler_params=pltpu.CompilerParams(vmem_limit_bytes=60 << 20),
        cost_estimate=pl.CostEstimate(
            flops=24 * count * slots * width * ff,
            transcendentals=count * slots * ff,
            bytes_accessed=4 * n * rows * width * 2 + 3 * count * width * ff * 2,
        ),
        name="experts",
    )(own.reshape(1), *blocks, *grads, pick, turned, router_turned, gate, up, down, *kept)
    return outs[:n], outs[n : 2 * n], outs[2 * n : 2 * n + 5], outs[2 * n + 5]


def turn(x):
    return pltpu.roll(x, HEAD // 2, 1)


def attend_kernel(n, tile, own_ref, *refs):
    xs = refs[:n]
    wq, wk, wv, gains_ref, cos_ref, sin_ref, seg_col, seg_row = refs[n : n + 8]
    attended_ref, normed_ref, raw_ref, low_ref = refs[n + 8 :]
    own = own_ref[0]
    rows, width = xs[0].shape
    part = wq.shape[1]
    group = n * rows
    for k in range(n):
        normed_ref[own ^ k] = xs[k][...]
    for r in range(0, group, tile):
        span = pl.ds(r, tile)
        block = normed_ref[r // rows : (r + tile) // rows].reshape(tile, width)
        cos, sin = cos_ref[span, :], sin_ref[span, :]
        for which, weight in enumerate((wq, wk, wv)):
            out = mm(block, weight[...])
            if which == 2:
                low_ref[span, 2 * part :] = out.astype(LOW)
                continue
            raw_ref[span, which * part : (which + 1) * part] = out
            for h in range(part // HEAD):
                x = out[:, h * HEAD : (h + 1) * HEAD]
                x = x * lax.rsqrt(jnp.mean(x * x, axis=1, keepdims=True) + EPS)
                x = x * gains_ref[which : which + 1, :]
                x = x * cos + turn(x) * sin
                at = which * part + h * HEAD
                low_ref[span, at : at + HEAD] = x.astype(LOW)
    for h in range(part // HEAD):
        keys = low_ref[:, part + h * HEAD : part + (h + 1) * HEAD]
        values = low_ref[:, 2 * part + h * HEAD : 2 * part + (h + 1) * HEAD]
        for r in range(0, group, tile):
            query = low_ref[r : r + tile, h * HEAD : (h + 1) * HEAD]
            scores = mm_nt(query, keys) * HEAD**-0.5
            same = seg_col[r : r + tile, :] == seg_row[...]
            scores = jnp.where(same, scores, NEGATIVE)
            terms = jnp.exp(scores - jnp.max(scores, axis=1, keepdims=True))
            probs = terms * (1.0 / jnp.sum(terms, axis=1, keepdims=True))
            out = mm(probs.astype(LOW), values).astype(LOW)
            for i in range(0, tile, rows):
                attended_ref[(r + i) // rows, :, h * HEAD : (h + 1) * HEAD] = out[i : i + rows]


def attend(own, blocks, qkv_weight, gains, cos, sin, seg, tile=512):
    n = len(blocks)
    rows, width = blocks[0].shape
    part = width // n
    group = n * rows

    def columns(which):
        return pl.BlockSpec((width, part), lambda i, o: (0, which * n + o[0]))

    def whole(*shape):
        return pl.BlockSpec(shape, lambda i, o: (0,) * len(shape))

    return pl.pallas_call(
        functools.partial(attend_kernel, n, tile),
        out_shape=[
            jax.ShapeDtypeStruct((n, rows, part), LOW),
            jax.ShapeDtypeStruct((n, rows, width), LOW),
            jax.ShapeDtypeStruct((group, 2 * part), F32),
            jax.ShapeDtypeStruct((group, 3 * part), LOW),
        ],
        grid_spec=pltpu.PrefetchScalarGridSpec(
            num_scalar_prefetch=1,
            grid=(1,),
            in_specs=[whole(rows, width)] * n
            + [columns(0), columns(1), columns(2)]
            + [
                whole(2, HEAD),
                whole(group, HEAD),
                whole(group, HEAD),
                whole(group, 1),
                whole(1, group),
            ],
            out_specs=[
                whole(n, rows, part),
                whole(n, rows, width),
                whole(group, 2 * part),
                whole(group, 3 * part),
            ],
        ),
        compiler_params=pltpu.CompilerParams(vmem_limit_bytes=56 << 20),
        cost_estimate=pl.CostEstimate(
            flops=2 * group * (3 * width * part + 2 * group * part),
            transcendentals=group * group * (part // HEAD),
            bytes_accessed=group * (4 * width + 18 * part) + 6 * width * part,
        ),
        name="attend",
    )(
        own.reshape(1),
        *blocks,
        qkv_weight,
        qkv_weight,
        qkv_weight,
        gains,
        cos,
        sin,
        seg[:, None],
        seg[None, :],
    )


def attend_back_kernel(
    n,
    tile,
    d_ref,
    low_ref,
    raw_ref,
    gains_ref,
    cos_ref,
    sin_ref,
    seg_col,
    seg_row,
    out_ref,
    gain_ref,
    dq_ref,
    dk_ref,
    dv_ref,
):
    rows, part = d_ref.shape[1:]
    group = n * rows
    scale = HEAD**-0.5
    gain_terms = [jnp.zeros((1, HEAD), F32), jnp.zeros((1, HEAD), F32)]
    for h in range(part // HEAD):
        cols = slice(h * HEAD, (h + 1) * HEAD)
        keys = low_ref[:, part + h * HEAD : part + (h + 1) * HEAD]
        values = low_ref[:, 2 * part + h * HEAD : 2 * part + (h + 1) * HEAD]
        for r in range(0, group, tile):
            query = low_ref[r : r + tile, cols]
            d_out = d_ref[r // rows : (r + tile) // rows, :, cols].reshape(tile, HEAD)
            scores = mm_nt(keys, query) * scale
            same = seg_col[...] == seg_row[:, r : r + tile]
            scores = jnp.where(same, scores, NEGATIVE)
            terms = jnp.exp(scores - jnp.max(scores, axis=0, keepdims=True))
            probs = terms * (1.0 / jnp.sum(terms, axis=0, keepdims=True))
            d_probs = mm_nt(values, d_out)
            delta = jnp.sum(probs * d_probs, axis=0, keepdims=True)
            d_scores = (probs * (d_probs - delta)).astype(LOW)
            dv = mm(probs.astype(LOW), d_out)
            dk = mm(d_scores, query)
            dq_ref[r : r + tile, :] = mm(d_scores, keys, ((0,), (0,))) * scale
            if r == 0:
                dv_ref[...] = dv
                dk_ref[...] = dk * scale
            else:
                dv_ref[...] += dv
                dk_ref[...] += dk * scale
        for r in range(0, group, rows):
            span = pl.ds(r, rows)
            cos, sin = cos_ref[span, :], sin_ref[span, :]
            at = 2 * part + h * HEAD
            out_ref[r // rows, :, at : at + HEAD] = dv_ref[span, :].astype(LOW)
            for which, grad_ref in enumerate((dq_ref, dk_ref)):
                at = which * part + h * HEAD
                raw = raw_ref[span, at : at + HEAD]
                inv = lax.rsqrt(jnp.mean(raw * raw, axis=1, keepdims=True) + EPS)
                unit = raw * inv
                grad = grad_ref[span, :]
                grad = grad * cos + turn(grad * sin)
                gain_terms[which] += jnp.sum(grad * unit, axis=0, keepdims=True)
                grad = grad * gains_ref[which : which + 1, :]
                grad = inv * (grad - unit * jnp.mean(grad * unit, axis=1, keepdims=True))
                out_ref[r // rows, :, at : at + HEAD] = grad.astype(LOW)
    for which in range(2):
        gain_ref[which : which + 1, :] = gain_terms[which]


def attend_back(d_attended, low, raw, gains, cos, sin, seg, tile=512):
    n, rows, part = d_attended.shape
    group = n * rows
    return pl.pallas_call(
        functools.partial(attend_back_kernel, n, tile),
        out_shape=[
            jax.ShapeDtypeStruct((n, rows, 3 * part), LOW),
            jax.ShapeDtypeStruct((2, HEAD), F32),
        ],
        scratch_shapes=[pltpu.VMEM((group, HEAD), F32)] * 3,
        compiler_params=pltpu.CompilerParams(vmem_limit_bytes=56 << 20),
        cost_estimate=pl.CostEstimate(
            flops=10 * group * group * part,
            transcendentals=group * group * (part // HEAD),
            bytes_accessed=group * part * 22,
        ),
        name="attend_back",
    )(d_attended, low, raw, gains, cos, sin, seg[:, None], seg[None, :])


def local(
    tokens,
    cotangent,
    qkv_weight,
    out_weight,
    router_weight,
    attn_gain,
    moe_gain,
    head_gains,
    gate_weight,
    up_weight,
    down_weight,
    permutation,
    lengths,
    routes,
):
    micro, rows, width = tokens.shape
    n = lax.axis_size("expert")
    m = lax.axis_size("shard")
    own = lax.axis_index("expert")
    own_shard = lax.axis_index("shard")
    local_count = gate_weight.shape[0]
    expert_count = local_count * n
    top_count = routes.shape[2]
    capacity = rows * top_count // expert_count
    part = width // n
    piece = width // (n * m)

    full_gate = lax.all_gather(gate_weight, "shard", axis=1, tiled=True)
    full_up = lax.all_gather(up_weight, "shard", axis=1, tiled=True)
    full_down = lax.all_gather(down_weight, "shard", axis=1, tiled=True)

    each = range(micro)
    routes_all = swap(jnp.broadcast_to(routes[None], (n,) + routes.shape), "expert")
    inputs = [tokens[i].astype(F32) for i in each]
    normed_attn = [rms_scale(x, attn_gain).astype(LOW) for x in inputs]
    normed_attn[0], routes_all = lax.optimization_barrier((normed_attn[0], routes_all))

    own_experts = own * local_count + jnp.arange(local_count, dtype=jnp.int32)
    by_micro = jnp.swapaxes(routes_all, 0, 1)
    hit = jnp.any(by_micro[None] == own_experts[:, None, None, None, None], axis=-1)
    hot = hit.astype(jnp.int32)
    slot = jnp.cumsum(hot, axis=-1) - hot
    slot_iota = jnp.arange(capacity, dtype=jnp.int32)
    pick = (hit[:, :, :, None, :] & (slot[:, :, :, None, :] == slot_iota[:, None])).astype(LOW)
    turned = (hit[..., None] & (slot[..., None] == slot_iota)).astype(LOW)

    gains = head_gains.reshape(2, HEAD)
    spots = [places(permutation[i, 0], lengths[i, 0]) for i in each]
    turns = [angles(pos) for _, pos in spots]
    near = [gather_first(x, "expert") for x in normed_attn]
    normed_blocks = [gather_second(x, "expert") for x in near]
    grad_near = [gather_first(tie(cotangent[i], near[-1][-2]), "expert") for i in each]
    attended, normed_all, qkv_raw, qkv_low, mixed, normed_moe = ([None] * micro for _ in range(6))
    for i in each:
        attended[i], normed_all[i], qkv_raw[i], qkv_low[i] = attend(
            own, normed_blocks[i], qkv_weight, gains, *turns[i], spots[i][0]
        )
        attended[i] = swap(attended[i], "expert")
        mixed[i] = inputs[i] + ein("hrp,hpd->rd", attended[i], out_weight.reshape(n, part, width))
        normed_moe[i] = rms_scale(mixed[i], moe_gain).astype(LOW)

    moe_sum, d_sum, d_gate = ([None] * micro for _ in range(3))
    kept = None
    for i in each:
        grad_blocks = gather_second(grad_near[i], "expert")
        moe_blocks = gather_blocks(normed_moe[i], "expert")
        moe_sum[i], d_sum[i], kept, d_gate[i] = expert_layer(
            own,
            moe_blocks,
            grad_blocks,
            pick,
            turned,
            router_weight.T,
            full_gate,
            full_up,
            full_down,
            i,
            micro,
            kept,
        )
    buffer, d_result, hidden, dg, du = kept
    gate_term = ein("erd,erf->edf", buffer, dg).astype(LOW)
    up_term = ein("erd,erf->edf", buffer, du).astype(LOW)
    down_term = ein("erf,erd->efd", hidden, d_result).astype(LOW)
    gate_grad, up_grad, down_grad = (
        lax.psum_scatter(term, "shard", scatter_dimension=1, tiled=True).astype(F32)
        for term in (gate_term, up_term, down_term)
    )

    output, input_grad, d_attn, d_qkv = ([None] * micro for _ in range(4))
    router_term, moe_gain_term, head_term, attn_gain_term = 0.0, 0.0, 0.0, 0.0
    for i in each:
        d_gates = swap(d_gate[i].transpose(1, 0, 2), "expert")
        d_router = d_gates.reshape(expert_count, rows).T
        d_normed = scatter_blocks(d_sum[i], "expert")
        grad_out = cotangent[i].astype(F32)
        logits = dot(normed_moe[i], router_weight)
        exp_logits = jnp.exp(logits - jnp.max(logits, axis=-1, keepdims=True))
        router = exp_logits / jnp.sum(exp_logits, axis=-1, keepdims=True)
        d_logits = (
            router * (d_router - jnp.sum(router * d_router, axis=-1, keepdims=True))
        ).astype(LOW)
        d_normed = d_normed + dot(d_logits, router_weight.T)
        router_term = router_term + dot(normed_moe[i].T, d_logits)
        _, norm_pull = jax.vjp(rms_scale, mixed[i], moe_gain)
        d_mixed_norm, term = norm_pull(d_normed)
        moe_gain_term = moe_gain_term + term
        d_mixed = grad_out + d_mixed_norm
        d_attn[i] = d_mixed.astype(LOW)
        d_attended = dot(d_attn[i], out_weight.T).astype(LOW)
        d_attended = swap(jnp.swapaxes(d_attended.reshape(rows, n, part), 0, 1), "expert")
        d_qkv[i], terms = attend_back(
            d_attended, qkv_low[i], qkv_raw[i], gains, *turns[i], spots[i][0]
        )
        head_term = head_term + terms.reshape(2 * HEAD)
        d_qkv_rows = swap(d_qkv[i], "expert").reshape(n, rows, 3, part).transpose(1, 2, 0, 3)
        d_normed_attn = dot(d_qkv_rows.reshape(rows, 3 * width), qkv_weight.T)
        _, attn_pull = jax.vjp(rms_scale, inputs[i], attn_gain)
        d_inputs_norm, term = attn_pull(d_normed_attn)
        attn_gain_term = attn_gain_term + term
        input_grad[i] = (d_mixed + d_inputs_norm).astype(LOW)
        moe_part = scatter_blocks([tie(x, d_normed) for x in moe_sum[i]], "expert")
        output[i] = (mixed[i] + moe_part).astype(LOW)

    attended_cols = jnp.stack([x.reshape(n, rows, m, piece) for x in attended])
    attended_cols = swap(attended_cols.transpose(3, 0, 2, 1, 4), "shard")
    attended_cols = attended_cols.reshape(m * micro * rows, n * piece)
    d_attn_all = place_blocks(
        gather_blocks(jnp.concatenate(d_attn, axis=0), "shard"), own_shard, 0
    )
    out_term = dot(attended_cols.T, d_attn_all).astype(LOW).reshape(n, piece, width)
    out_grad = scatter_blocks(
        [x[0] for x in take_blocks(out_term, own, n, 0)], "expert"
    )

    qkv_term = sum(
        dot(normed_all[i].reshape(n * rows, width).T, d_qkv[i].reshape(n * rows, 3 * part))
        for i in each
    ).astype(LOW)
    qkv_term = jnp.swapaxes(qkv_term.reshape(n, m, piece, 3 * part), 0, 1)
    qkv_sum = scatter_blocks(take_blocks(qkv_term, own_shard, m, 0), "shard").astype(LOW)
    qkv_rows = swap(qkv_sum.reshape(n, piece, 3 * part), "expert")
    qkv_grad = (
        qkv_rows.reshape(n, piece, 3, part).transpose(1, 2, 0, 3).reshape(piece, 3 * width)
    ).astype(F32)
    output, input_grad = jnp.stack(output), jnp.stack(input_grad)

    world = n * m
    head_piece = 2 * HEAD // world
    small = jnp.concatenate(
        [
            router_term.reshape(world, piece * expert_count),
            attn_gain_term.reshape(world, piece),
            moe_gain_term.reshape(world, piece),
            head_term.reshape(world, head_piece),
        ],
        axis=1,
    )
    used = small.shape[1]
    padded = -(-used // 1024) * 1024
    small = jnp.pad(small, ((0, 0), (0, padded - used))).reshape(world, padded // 128, 128)
    small = jnp.sum(swap(small, ("expert", "shard")), axis=0).reshape(padded)
    a = piece * expert_count
    return (
        output,
        input_grad,
        qkv_grad,
        out_grad,
        small[:a].reshape(piece, expert_count),
        small[a : a + piece],
        small[a + piece : a + 2 * piece],
        small[a + 2 * piece : a + 2 * piece + head_piece],
        gate_grad,
        up_grad,
        down_grad,
    )


def solution(mesh):
    return jax.shard_map(
        local,
        mesh=mesh,
        in_specs=(
            P(None, ("expert", "shard"), None),
            P(None, ("expert", "shard"), None),
            P(),
            P(),
            P(),
            P(),
            P(),
            P(),
            P("expert", "shard", None),
            P("expert", "shard", None),
            P("expert", "shard", None),
            P(None, "shard", None),
            P(None, "shard", None),
            P(None, ("expert", "shard"), None),
        ),
        out_specs=(
            P(None, ("expert", "shard"), None),
            P(None, ("expert", "shard"), None),
            P(("expert", "shard"), None),
            P(("expert", "shard"), None),
            P(("expert", "shard"), None),
            P(("expert", "shard")),
            P(("expert", "shard")),
            P(("expert", "shard")),
            P("expert", "shard", None),
            P("expert", "shard", None),
            P("expert", "shard", None),
        ),
        check_vma=False,
    )
```

```python
import functools

import jax
import jax.numpy as jnp
from jax import lax
from jax.experimental import pallas as pl
from jax.experimental.pallas import tpu as pltpu
from jax.sharding import PartitionSpec as P

HEAD = 128
EPS = 1e-06
ROPE_BASE = 10000.0
NEGATIVE = -1e30
LOW = jnp.bfloat16
F32 = jnp.float32


def rms_scale(values, gain_vec):
    return values * lax.rsqrt(jnp.mean(values * values, axis=-1, keepdims=True) + EPS) * gain_vec


def places(perm_row, length_row):
    seq_ends = jnp.cumsum(length_row)
    seg_ids = jnp.sum((perm_row[:, None] >= seq_ends[None, :]).astype(jnp.int32), axis=1)
    starts = seq_ends - length_row
    pick_mask = seg_ids[:, None] == jnp.arange(length_row.shape[0], dtype=jnp.int32)[None, :]
    seq_begin = jnp.sum(jnp.where(pick_mask, starts[None, :], 0), axis=1)
    return (seg_ids, perm_row - seq_begin)


def angles(positions):
    half_size = HEAD // 2
    frequency = jnp.power(ROPE_BASE, -2.0 * jnp.arange(half_size, dtype=F32) / HEAD)
    turned = positions.astype(F32)[..., None] * frequency
    cosine, sine = jnp.cos(turned), jnp.sin(turned)
    return (
        jnp.concatenate([cosine, cosine], axis=-1),
        jnp.concatenate([-sine, sine], axis=-1),
    )


def hop(value, axis, step):
    size = lax.axis_size(axis)
    return lax.ppermute(value, axis, [(i, i ^ step) for i in range(size)])


def gather_first(value, axis):
    size = lax.axis_size(axis)
    blocks = [None] * size
    blocks[0] = value
    for k in range(2, size, 2):
        blocks[k] = hop(value, axis, k)
    return blocks


def gather_second(blocks, axis):
    blocks = list(blocks)
    for k in range(0, len(blocks), 2):
        blocks[k + 1] = hop(blocks[k], axis, 1)
    return blocks


def gather_blocks(value, axis):
    return gather_second(gather_first(value, axis), axis)


def far_sum(half, received):
    return half[0].astype(F32) + sum(x.astype(F32) for x in received)


def near_sums(keep, received):
    return [(k.astype(F32) + r.astype(F32)).astype(LOW) for k, r in zip(keep, received)]


def far_sends(half, after):
    return [hop(tie(half[j], *after), "expert", 2 * j) for j in range(1, len(half))]


def scatter_blocks(blocks, axis):
    half = [
        (blocks[k].astype(F32) + hop(blocks[k + 1], axis, 1).astype(F32)).astype(LOW)
        for k in range(0, len(blocks), 2)
    ]
    return far_sum(half, [hop(half[j], axis, 2 * j) for j in range(1, len(half))])


def place_blocks(blocks, own, dim):
    size = blocks[0].shape[dim]
    shape = list(blocks[0].shape)
    shape[dim] = size * len(blocks)
    whole = jnp.zeros(shape, blocks[0].dtype)
    for k, block in enumerate(blocks):
        whole = lax.dynamic_update_slice_in_dim(whole, block, (own ^ k) * size, dim)
    return whole


def take_blocks(whole, own, count, dim):
    size = whole.shape[dim] // count
    return [lax.dynamic_slice_in_dim(whole, (own ^ k) * size, size, dim) for k in range(count)]


def swap(value, axis):
    return lax.all_to_all(value, axis, split_axis=0, concat_axis=0, tiled=True)


def dot(a, b):
    return jnp.dot(a, b, preferred_element_type=F32)


def ein(spec, a, b):
    return jnp.einsum(spec, a, b, preferred_element_type=F32)


def tie(value, *others):
    return lax.optimization_barrier((value, others))[0]


def mm(a, b, dims=((1,), (0,))):
    return lax.dot_general(a, b, (dims, ((), ())), preferred_element_type=F32)


def mm_nt(a, b):
    return mm(a, b, ((1,), (1,)))


def expert_kernel(n, tile, grads_near, shared, own_ref, *refs):
    refs = list(refs)

    def take(count):
        out = refs[:count]
        del refs[:count]
        return out

    near, (far_ref,) = take(n // 2), take(1)
    grads = take(n // 2 + 1) if grads_near else take(1)
    pick_ref, turned_ref, router_ref, gate_ref, up_ref, down_ref = take(6)
    take(shared)
    buffer_ref, d_result_ref, hidden_ref, dg_ref, du_ref, moe_ref = take(6)
    d_keep, d_send = take(2)
    acc_res, acc_db, grad_rows, gate_cols = take(4)
    own = own_ref[0]
    expert, step, steps = pl.program_id(0), pl.program_id(1), pl.num_programs(1)
    count = pl.num_programs(0)
    cap, rows = pick_ref.shape[3:]
    width = acc_res.shape[1]
    index = own * count + expert

    @pl.when(step == 0)
    def _():
        for k in range(n):
            span = pl.ds(k * cap, cap)
            block = far_ref[k // 2] if k % 2 else near[k // 2][...]
            pick = pick_ref[0, 0, own ^ k]
            buffer_ref[0, span, :] = mm(pick, block).astype(LOW)
            logits = mm_nt(router_ref[...], block)
            terms = jnp.exp(logits - jnp.max(logits, axis=0, keepdims=True))
            router = terms / jnp.sum(terms, axis=0, keepdims=True)
            lines = lax.broadcasted_iota(jnp.int32, router.shape, 0)
            row = jnp.sum(jnp.where(lines == index, router, 0.0), axis=0, keepdims=True)
            col = jnp.sum(pick.astype(F32) * row, axis=1, keepdims=True)
            if grads_near:
                block = grads[-1][k // 2] if k % 2 else grads[k // 2][...]
            else:
                block = grads[0][own ^ k]
            block = mm(pick, block)
            grad_rows[span, :] = block.astype(LOW)
            d_result_ref[0, span, :] = (col * block).astype(LOW)
            gate_cols[span, :] = jnp.broadcast_to(col, (cap, gate_cols.shape[1]))

    slots = n * cap
    for r in range(0, slots, tile):
        span = pl.ds(r, tile)
        rows_in = buffer_ref[0, span, :]
        gate_act = mm(rows_in, gate_ref[0])
        up_act = mm(rows_in, up_ref[0])
        d_hidden = mm_nt(d_result_ref[0, span, :], down_ref[0])
        sig = 1.0 / (1.0 + jnp.exp(-gate_act))
        silu = gate_act * sig
        hidden_ref[0, span, :] = (silu * up_act).astype(LOW)
        slope = sig * (1.0 + gate_act * (1.0 - sig))
        dg_ref[0, span, :] = (d_hidden * up_act * slope).astype(LOW)
        du_ref[0, span, :] = (d_hidden * silu).astype(LOW)

        @pl.when(step == 0)
        def _():
            acc_res[span, :] = mm(hidden_ref[0, span, :], down_ref[0])
            acc_db[span, :] = mm_nt(dg_ref[0, span, :], gate_ref[0]) + mm_nt(
                du_ref[0, span, :], up_ref[0]
            )

        @pl.when(step > 0)
        def _():
            acc_res[span, :] += mm(hidden_ref[0, span, :], down_ref[0])
            acc_db[span, :] += mm_nt(dg_ref[0, span, :], gate_ref[0]) + mm_nt(
                du_ref[0, span, :], up_ref[0]
            )

    @pl.when(step == steps - 1)
    def _():
        lines = count * n * rows // width
        place = index * rows
        line, column = place // width, place % width
        shape = (d_keep.shape[1] - rows, width)
        at_line = lax.broadcasted_iota(jnp.int32, shape, 0)
        at_column = lax.broadcasted_iota(jnp.int32, shape, 1)
        here = (at_column >= column) & (at_column < column + rows)
        for k in range(n):
            span = pl.ds(k * cap, cap)
            out = d_send if k % 2 else d_keep
            pick = pick_ref[0, 0, own ^ k]
            turned = turned_ref[0, 0, own ^ k]
            result = acc_res[span, :].astype(LOW).astype(F32)
            col = jnp.sum(result * grad_rows[span, :].astype(F32), axis=1, keepdims=True)
            row = jnp.sum(pick.astype(F32) * col, axis=0, keepdims=True)
            high = row.astype(LOW).astype(F32)
            high, rest = (
                jnp.concatenate([x] * (width // rows), axis=1) for x in (high, row - high)
            )
            extra = jnp.where(here & (at_line == line), high, 0.0) + jnp.where(
                here & (at_line == line + lines), rest, 0.0
            )
            part = mm(turned, (gate_cols[span, :1] * result).astype(LOW))
            d_part = mm(turned, acc_db[span, :].astype(LOW))

            @pl.when(expert == 0)
            def _():
                moe_ref[own ^ k, 0] = part.astype(LOW)
                out[k // 2, :rows] = d_part.astype(LOW)
                out[k // 2, rows:] = extra.astype(LOW)

            @pl.when(expert > 0)
            def _():
                moe_ref[own ^ k, 0] = (moe_ref[own ^ k, 0].astype(F32) + part).astype(LOW)
                out[k // 2, :rows] = (out[k // 2, :rows].astype(F32) + d_part).astype(LOW)
                out[k // 2, rows:] = (out[k // 2, rows:].astype(F32) + extra).astype(LOW)


def expert_layer(own, blocks, far, grads, pick, turned, router_turned, weights, at, micro, kept):
    n = 2 * len(blocks)
    rows, width = blocks[0].shape
    count, _, ff = weights[0].shape
    cap = pick.shape[3]
    slots = n * cap
    split = 2 if n <= 8 else 4
    ft = ff // split
    extra = 8
    one = dict(pipeline_mode=pl.Buffered(1))
    some = one if n > 8 else {}
    block = pl.BlockSpec((rows, width), lambda e, f, o: (0, 0), **one)

    def stack(size, height):
        return pl.BlockSpec((size, height, width), lambda e, f, o: (0, 0, 0), **one)

    row_block = pl.BlockSpec((1, slots, width), lambda e, f, o: (e, at, 0), **some)
    ff_block = pl.BlockSpec((1, slots, ft), lambda e, f, o: (e, at, f))
    rows_shape = jax.ShapeDtypeStruct((count, micro * slots, width), LOW)
    ff_shape = jax.ShapeDtypeStruct((count, micro * slots, ff), LOW)
    grads_near = len(grads) > 1
    kept = [] if kept is None else list(kept)
    args = [*blocks, far, *grads, pick, turned, router_turned, *weights]
    outs = pl.pallas_call(
        functools.partial(expert_kernel, n, 512, grads_near, len(kept)),
        out_shape=[rows_shape, rows_shape, ff_shape, ff_shape, ff_shape]
        + [jax.ShapeDtypeStruct((n, micro, rows, width), LOW)]
        + [jax.ShapeDtypeStruct((n // 2, rows + extra, width), LOW)] * 2,
        grid_spec=pltpu.PrefetchScalarGridSpec(
            num_scalar_prefetch=1,
            grid=(count, split),
            in_specs=[block] * (n // 2)
            + [stack(n // 2, rows)]
            + ([block] * (n // 2) + [stack(n // 2, rows)] if grads_near else [stack(n, rows)])
            + [
                pl.BlockSpec((1, 1, n, cap, rows), lambda e, f, o: (e, at, 0, 0, 0), **some),
                pl.BlockSpec((1, 1, n, rows, cap), lambda e, f, o: (e, at, 0, 0, 0), **some),
                pl.BlockSpec(router_turned.shape, lambda e, f, o: (0, 0)),
                pl.BlockSpec((1, width, ft), lambda e, f, o: (e, 0, f)),
                pl.BlockSpec((1, width, ft), lambda e, f, o: (e, 0, f)),
                pl.BlockSpec((1, ft, width), lambda e, f, o: (e, f, 0)),
            ]
            + [pl.BlockSpec(memory_space=pl.ANY)] * len(kept),
            out_specs=[row_block, row_block, ff_block, ff_block, ff_block]
            + [pl.BlockSpec((n, 1, rows, width), lambda e, f, o: (0, at, 0, 0), **one)]
            + [stack(n // 2, rows + extra)] * 2,
            scratch_shapes=[
                pltpu.VMEM((slots, width), F32),
                pltpu.VMEM((slots, width), F32),
                pltpu.VMEM((slots, width), LOW),
                pltpu.VMEM((slots, 128), F32),
            ],
        ),
        input_output_aliases={1 + len(args) + i: i for i in range(len(kept))},
        compiler_params=pltpu.CompilerParams(vmem_limit_bytes=60 << 20),
        cost_estimate=pl.CostEstimate(
            flops=24 * count * slots * width * ff,
            transcendentals=count * slots * ff,
            bytes_accessed=4 * n * rows * width * 2 + 3 * count * width * ff * 2,
        ),
        name="experts",
    )(own.reshape(1), *args, *kept)
    return outs[:6], outs[6], outs[7]


def turn(x):
    return pltpu.roll(x, HEAD // 2, 1)


def attend_kernel(n, tile, own_ref, *refs):
    xs = refs[:n]
    wq, wk, wv, gains_ref, cos_ref, sin_ref, seg_col, seg_row = refs[n : n + 8]
    attended_ref, normed_ref, raw_ref, low_ref = refs[-4:]
    own = own_ref[0]
    rows, width = xs[0].shape
    part = wq.shape[1]
    group = n * rows
    for k in range(n):
        normed_ref[own ^ k] = xs[k][...]
    for r in range(0, group, tile):
        span = pl.ds(r, tile)
        block = normed_ref[r // rows : (r + tile) // rows].reshape(tile, width)
        cos, sin = cos_ref[span, :], sin_ref[span, :]
        for which, weight in enumerate((wq, wk, wv)):
            out = mm(block, weight[...])
            if which == 2:
                low_ref[span, 2 * part :] = out.astype(LOW)
                continue
            raw_ref[span, which * part : (which + 1) * part] = out
            for h in range(part // HEAD):
                x = out[:, h * HEAD : (h + 1) * HEAD]
                x = x * lax.rsqrt(jnp.mean(x * x, axis=1, keepdims=True) + EPS)
                x = x * gains_ref[which : which + 1, :]
                x = x * cos + turn(x) * sin
                at = which * part + h * HEAD
                low_ref[span, at : at + HEAD] = x.astype(LOW)
    for h in range(part // HEAD):
        keys = low_ref[:, part + h * HEAD : part + (h + 1) * HEAD]
        values = low_ref[:, 2 * part + h * HEAD : 2 * part + (h + 1) * HEAD]
        for r in range(0, group, tile):
            query = low_ref[r : r + tile, h * HEAD : (h + 1) * HEAD]
            scores = mm_nt(query, keys) * HEAD**-0.5
            same = seg_col[r : r + tile, :] == seg_row[...]
            scores = jnp.where(same, scores, NEGATIVE)
            terms = jnp.exp(scores - jnp.max(scores, axis=1, keepdims=True))
            probs = terms * (1.0 / jnp.sum(terms, axis=1, keepdims=True))
            out = mm(probs.astype(LOW), values).astype(LOW)
            for i in range(0, tile, rows):
                attended_ref[(r + i) // rows, :rows, h * HEAD : (h + 1) * HEAD] = out[
                    i : i + rows
                ]
    if len(refs) > n + 12:
        for k in range(n):
            attended_ref[k, rows:, :] = refs[n + 8][...]


def attend(own, blocks, qkv_weight, gains, cos, sin, seg, riders, tile=512):
    n = len(blocks)
    rows, width = blocks[0].shape
    part = width // n
    group = n * rows
    more = sum(x.shape[0] for x in riders)

    def columns(which):
        return pl.BlockSpec((width, part), lambda i, o: (0, which * n + o[0]))

    def whole(*shape):
        return pl.BlockSpec(shape, lambda i, o: (0,) * len(shape))

    return pl.pallas_call(
        functools.partial(attend_kernel, n, tile),
        out_shape=[
            jax.ShapeDtypeStruct((n, rows + more, part), LOW),
            jax.ShapeDtypeStruct((n, rows, width), LOW),
            jax.ShapeDtypeStruct((group, 2 * part), F32),
            jax.ShapeDtypeStruct((group, 3 * part), LOW),
        ],
        grid_spec=pltpu.PrefetchScalarGridSpec(
            num_scalar_prefetch=1,
            grid=(1,),
            in_specs=[whole(rows, width)] * n
            + [columns(0), columns(1), columns(2)]
            + [
                whole(2, HEAD),
                whole(group, HEAD),
                whole(group, HEAD),
                whole(group, 1),
                whole(1, group),
            ]
            + [whole(*x.shape) for x in riders],
            out_specs=[
                whole(n, rows + more, part),
                whole(n, rows, width),
                whole(group, 2 * part),
                whole(group, 3 * part),
            ],
        ),
        compiler_params=pltpu.CompilerParams(vmem_limit_bytes=56 << 20),
        cost_estimate=pl.CostEstimate(
            flops=2 * group * (3 * width * part + 2 * group * part),
            transcendentals=group * group * (part // HEAD),
            bytes_accessed=group * (4 * width + 18 * part) + 6 * width * part,
        ),
        name="attend",
    )(
        own.reshape(1),
        *blocks,
        qkv_weight,
        qkv_weight,
        qkv_weight,
        gains,
        cos,
        sin,
        seg[:, None],
        seg[None, :],
        *riders,
    )


def attend_back_kernel(
    n,
    tile,
    d_ref,
    low_ref,
    raw_ref,
    gains_ref,
    cos_ref,
    sin_ref,
    seg_col,
    seg_row,
    out_ref,
    gain_ref,
    dq_ref,
    dk_ref,
    dv_ref,
):
    rows, part = d_ref.shape[1:]
    group = n * rows
    scale = HEAD**-0.5
    gain_terms = [jnp.zeros((1, HEAD), F32), jnp.zeros((1, HEAD), F32)]
    for h in range(part // HEAD):
        cols = slice(h * HEAD, (h + 1) * HEAD)
        keys = low_ref[:, part + h * HEAD : part + (h + 1) * HEAD]
        values = low_ref[:, 2 * part + h * HEAD : 2 * part + (h + 1) * HEAD]
        for r in range(0, group, tile):
            query = low_ref[r : r + tile, cols]
            d_out = d_ref[r // rows : (r + tile) // rows, :, cols].reshape(tile, HEAD)
            scores = mm_nt(keys, query) * scale
            same = seg_col[...] == seg_row[:, r : r + tile]
            scores = jnp.where(same, scores, NEGATIVE)
            terms = jnp.exp(scores - jnp.max(scores, axis=0, keepdims=True))
            probs = terms * (1.0 / jnp.sum(terms, axis=0, keepdims=True))
            d_probs = mm_nt(values, d_out)
            delta = jnp.sum(probs * d_probs, axis=0, keepdims=True)
            d_scores = (probs * (d_probs - delta)).astype(LOW)
            dv = mm(probs.astype(LOW), d_out)
            dk = mm(d_scores, query)
            dq_ref[r : r + tile, :] = mm(d_scores, keys, ((0,), (0,))) * scale
            if r == 0:
                dv_ref[...] = dv
                dk_ref[...] = dk * scale
            else:
                dv_ref[...] += dv
                dk_ref[...] += dk * scale
        for r in range(0, group, rows):
            span = pl.ds(r, rows)
            cos, sin = cos_ref[span, :], sin_ref[span, :]
            at = 2 * part + h * HEAD
            out_ref[r // rows, :, at : at + HEAD] = dv_ref[span, :].astype(LOW)
            for which, grad_ref in enumerate((dq_ref, dk_ref)):
                at = which * part + h * HEAD
                raw = raw_ref[span, at : at + HEAD]
                inv = lax.rsqrt(jnp.mean(raw * raw, axis=1, keepdims=True) + EPS)
                unit = raw * inv
                grad = grad_ref[span, :]
                grad = grad * cos + turn(grad * sin)
                gain_terms[which] += jnp.sum(grad * unit, axis=0, keepdims=True)
                grad = grad * gains_ref[which : which + 1, :]
                grad = inv * (grad - unit * jnp.mean(grad * unit, axis=1, keepdims=True))
                out_ref[r // rows, :, at : at + HEAD] = grad.astype(LOW)
    for which in range(2):
        gain_ref[which : which + 1, :] = gain_terms[which]


def attend_back(d_attended, low, raw, gains, cos, sin, seg, tile=512):
    n, rows, part = d_attended.shape
    group = n * rows
    return pl.pallas_call(
        functools.partial(attend_back_kernel, n, tile),
        out_shape=[
            jax.ShapeDtypeStruct((n, rows, 3 * part), LOW),
            jax.ShapeDtypeStruct((2, HEAD), F32),
        ],
        scratch_shapes=[pltpu.VMEM((group, HEAD), F32)] * 3,
        compiler_params=pltpu.CompilerParams(vmem_limit_bytes=56 << 20),
        cost_estimate=pl.CostEstimate(
            flops=10 * group * group * part,
            transcendentals=group * group * (part // HEAD),
            bytes_accessed=group * part * 22,
        ),
        name="attend_back",
    )(d_attended, low, raw, gains, cos, sin, seg[:, None], seg[None, :])


def local(
    tokens,
    cotangent,
    qkv_weight,
    out_weight,
    router_weight,
    attn_gain,
    moe_gain,
    head_gains,
    gate_weight,
    up_weight,
    down_weight,
    permutation,
    lengths,
    routes,
):
    micro, rows, width = tokens.shape
    n = lax.axis_size("expert")
    m = lax.axis_size("shard")
    own = lax.axis_index("expert")
    own_shard = lax.axis_index("shard")
    local_count = gate_weight.shape[0]
    expert_count = local_count * n
    top_count = routes.shape[2]
    capacity = rows * top_count // expert_count
    part = width // n
    piece = width // (n * m)

    full_gate = lax.all_gather(gate_weight, "shard", axis=1, tiled=True)
    full_up = lax.all_gather(up_weight, "shard", axis=1, tiled=True)
    full_down = lax.all_gather(down_weight, "shard", axis=1, tiled=True)

    each = range(micro)
    inputs = [tokens[i].astype(F32) for i in each]
    normed_attn = [rms_scale(x, attn_gain).astype(LOW) for x in inputs]
    near = [gather_first(normed_attn[0], "expert")]
    for i in range(1, micro):
        near.append(gather_first(tie(normed_attn[i], near[i - 1][2]), "expert"))
    gains = head_gains.reshape(2, HEAD)
    spots = [places(permutation[i, 0], lengths[i, 0]) for i in each]
    turns = [angles(pos) for _, pos in spots]
    normed_blocks = [gather_second(x, "expert") for x in near]
    grad_near = gather_first(tie(cotangent[0], *near[-1][2::2]), "expert")[::2]
    grad_far = hop(jnp.stack(grad_near), "expert", 1)
    grad_rest = [
        lax.all_gather(tie(cotangent[i], near[-1][-2]), "expert", axis=0) for i in range(1, micro)
    ]
    attended, normed_all, qkv_raw, qkv_low, mixed, normed_moe = ([None] * micro for _ in range(6))
    for i in each:
        riders = ()
        if i == 0:
            riders = (routes.astype(LOW).transpose(0, 2, 1).reshape(-1, part),)
        attended[i], normed_all[i], qkv_raw[i], qkv_low[i] = attend(
            own, normed_blocks[i], qkv_weight, gains, *turns[i], spots[i][0], riders
        )
        attended[i] = swap(attended[i], "expert")
        if i == 0:
            routes_all = attended[i][:, rows:]
            attended[i] = attended[i][:, :rows]
        elif i == 1:
            attended[i] = tie(attended[i], *grad_near[1:])
        mixed[i] = inputs[i] + ein("hrp,hpd->rd", attended[i], out_weight.reshape(n, part, width))
        normed_moe[i] = rms_scale(mixed[i], moe_gain).astype(LOW)
    attended_cols = jnp.stack([x.reshape(n, rows, m, piece) for x in attended])
    attended_cols = swap(attended_cols.transpose(3, 0, 2, 1, 4), "shard")
    attended_cols = attended_cols.reshape(m * micro * rows, n * piece)

    own_experts = own * local_count + jnp.arange(local_count, dtype=jnp.int32)
    by_micro = routes_all.reshape(n, micro, top_count, rows).swapaxes(0, 1).astype(jnp.int32)
    hit = jnp.any(by_micro[None] == own_experts[:, None, None, None, None], axis=3)
    hot = hit.astype(jnp.int32)
    slot = jnp.cumsum(hot, axis=-1) - hot
    slot_iota = jnp.arange(capacity, dtype=jnp.int32)
    pick = (hit[:, :, :, None, :] & (slot[:, :, :, None, :] == slot_iota[:, None])).astype(LOW)
    turned = (hit[..., None] & (slot[..., None] == slot_iota)).astype(LOW)

    weights = (full_gate, full_up, full_down)
    moe_near, moe_far = ([None] * micro for _ in range(2))
    for i in each:
        ready = tie(normed_moe[i], grad_far, *moe_near[i - 1][1:]) if i else normed_moe[i]
        moe_near[i] = gather_first(ready, "expert")[::2]
    moe_far[0] = jnp.stack([hop(x, "expert", 1) for x in moe_near[0]])
    grads = [(*grad_near, grad_far)] + [(x,) for x in grad_rest]
    kept, wait = None, (attended_cols, *moe_near[-1][1:])
    keep, received = ([None] * micro for _ in range(2))
    for i in each:
        if i:
            moe_far[i] = hop(jnp.stack(moe_near[i]), "expert", 1)
        kept, keep[i], send = expert_layer(
            own,
            [tie(moe_near[i][0], *wait)] + moe_near[i][1:],
            moe_far[i],
            grads[i],
            pick,
            turned,
            router_weight.T,
            weights,
            i,
            micro,
            kept,
        )
        received[i] = hop(send, "expert", 1)
        wait = ()
    buffer, d_result, hidden, dg, du, moe_sum = kept
    def grad_rows(term):
        return lax.psum_scatter(term, "shard", scatter_dimension=1, tiled=True)

    gate_term = ein("erd,erf->edf", buffer, dg).astype(LOW)
    up_term = ein("erd,erf->edf", buffer, tie(du, gate_term)).astype(LOW)
    half, far = [None] * micro, [None] * micro

    d_attn, d_attended, d_mixed, d_qkv, d_qkv_sent = ([None] * micro for _ in range(5))
    head_terms = [None] * micro
    router_term, moe_gain_term = 0.0, 0.0
    for i in each:
        half[i] = near_sums(
            keep[i], tie(received[i], *(d_attended[i - 1], up_term) if i else (buffer,))
        )
        far[i] = far_sends(half[i], ())
        if i:
            gate_grad = lax.psum_scatter(
                tie(gate_term, half[i][0]), "shard", scatter_dimension=1, tiled=True
            )
        total = far_sum(half[i], far[i])
        if i == 0:
            total = tie(total, gate_term)
        if i:
            down_term = ein("erf,erd->efd", tie(hidden, half[i][0]), d_result).astype(LOW)
            total = tie(total, d_qkv[i - 1], down_term)
        d_normed = total[:rows]
        lines = expert_count * rows // width
        d_router = total[rows : rows + lines] + total[rows + lines : rows + 2 * lines]
        d_router = d_router.reshape(expert_count, rows).T
        grad_out = cotangent[i].astype(F32)
        logits = dot(normed_moe[i], router_weight)
        exp_logits = jnp.exp(logits - jnp.max(logits, axis=-1, keepdims=True))
        router = exp_logits / jnp.sum(exp_logits, axis=-1, keepdims=True)
        d_logits = (
            router * (d_router - jnp.sum(router * d_router, axis=-1, keepdims=True))
        ).astype(LOW)
        d_normed = d_normed + dot(d_logits, router_weight.T)
        router_term = router_term + dot(normed_moe[i].T, d_logits)
        _, norm_pull = jax.vjp(rms_scale, mixed[i], moe_gain)
        d_mixed_norm, term = norm_pull(d_normed)
        moe_gain_term = moe_gain_term + term
        d_mixed[i] = grad_out + d_mixed_norm
        d_attn[i] = d_mixed[i].astype(LOW)
        back = dot(d_attn[i], out_weight.T).astype(LOW)
        back = jnp.swapaxes(back.reshape(rows, n, part), 0, 1)
        d_attended[i] = swap(tie(back, d_qkv_sent[i - 1]) if i else back, "expert")
        d_qkv[i], head_terms[i] = attend_back(
            d_attended[i], qkv_low[i], qkv_raw[i], gains, *turns[i], spots[i][0]
        )
        d_qkv_sent[i] = swap(d_qkv[i], "expert")

    moe_part = lax.psum_scatter(
        tie(moe_sum, d_attended[-1]).reshape(n * micro * rows, width),
        "expert",
        scatter_dimension=0,
        tiled=True,
    ).reshape(micro, rows, width)

    up_grad = scatter_blocks(take_blocks(tie(up_term, d_qkv[-1]), own_shard, m, 1), "shard")

    down_grad = scatter_blocks(
        take_blocks(tie(down_term, d_qkv[-1]), own_shard, m, 1), "shard"
    )

    d_attn_all = place_blocks(
        gather_blocks(tie(jnp.concatenate(d_attn, axis=0), d_qkv[-1]), "shard"), own_shard, 0
    )
    out_term = dot(tie(attended_cols, d_qkv[-1]).T, d_attn_all)
    out_term = out_term.astype(LOW)
    parts = take_blocks(out_term, own, n, 0)
    out_near = hop(jnp.stack(parts[1::2]), "expert", 1)
    out_half = near_sums(parts[::2], out_near)
    out_grad = far_sum(out_half, far_sends(out_half, ()))
    head_term = sum(head_terms).reshape(2 * HEAD)

    def input_gradient(i, *wait):
        sent = d_qkv_sent[i].reshape(n, rows, 3, part).transpose(1, 2, 0, 3)
        d_normed_attn = dot(tie(sent.reshape(rows, 3 * width), *wait), qkv_weight.T)
        _, pull = jax.vjp(lambda x: rms_scale(x, attn_gain), inputs[i])
        return (d_mixed[i] + pull(d_normed_attn)[0]).astype(LOW)

    qkv_term = sum(
        dot(normed_all[i].reshape(n * rows, width).T, d_qkv[i].reshape(n * rows, 3 * part))
        for i in reversed(each)
    ).astype(LOW)
    qkv_term = jnp.swapaxes(qkv_term.reshape(n, m, piece, 3 * part), 0, 1)
    parts = take_blocks(qkv_term, own_shard, m, 0)
    qkv_half = [
        (parts[k].astype(F32) + hop(parts[k + 1], "shard", 1).astype(F32)).astype(LOW)
        for k in range(0, m, 2)
    ]
    qkv_far = [hop(qkv_half[j], "shard", 2 * j) for j in range(1, m // 2)]
    gate_grad, up_grad, down_grad = (x.astype(F32) for x in (gate_grad, up_grad, down_grad))
    input_grad = [input_gradient(i, qkv_half[0]) for i in range(micro - 1)]
    qkv_sum = far_sum(qkv_half, qkv_far).astype(LOW)
    qkv_sum = tie(qkv_sum, d_qkv_sent[-1], *input_grad)
    qkv_rows = swap(qkv_sum.reshape(n, piece, 3 * part), "expert")
    qkv_grad = (
        qkv_rows.reshape(n, piece, 3, part).transpose(1, 2, 0, 3).reshape(piece, 3 * width)
    ).astype(F32)
    input_grad.append(input_gradient(micro - 1, qkv_sum))
    output = [(mixed[i] + moe_part[i].astype(F32)).astype(LOW) for i in each]
    output, input_grad = jnp.stack(output), jnp.stack(input_grad)

    first = (own * m + own_shard) * piece
    own_rows = lax.dynamic_slice_in_dim(qkv_weight, first, piece, 0).astype(F32)
    own_gain = lax.dynamic_slice_in_dim(attn_gain, first, piece, 0)
    attn_gain_grad = jnp.sum(qkv_grad * own_rows, axis=1) / own_gain

    world = n * m
    head_piece = 2 * HEAD // world
    small = jnp.concatenate(
        [
            router_term.reshape(world, piece * expert_count),
            moe_gain_term.reshape(world, piece),
            head_term.reshape(world, head_piece),
        ],
        axis=1,
    )
    used = small.shape[1]
    padded = -(-used // 1024) * 1024
    small = jnp.pad(small, ((0, 0), (0, padded - used))).reshape(world, padded // 128, 128)
    small = tie(small, d_qkv_sent[-1])
    small = jnp.sum(swap(small, ("expert", "shard")), axis=0).reshape(padded)
    a = piece * expert_count
    return (
        output,
        input_grad,
        qkv_grad,
        out_grad,
        small[:a].reshape(piece, expert_count),
        attn_gain_grad,
        small[a : a + piece],
        small[a + piece : a + piece + head_piece],
        gate_grad,
        up_grad,
        down_grad,
    )


def solution(mesh):
    return jax.shard_map(
        local,
        mesh=mesh,
        in_specs=(
            P(None, ("expert", "shard"), None),
            P(None, ("expert", "shard"), None),
            P(),
            P(),
            P(),
            P(),
            P(),
            P(),
            P("expert", "shard", None),
            P("expert", "shard", None),
            P("expert", "shard", None),
            P(None, "shard", None),
            P(None, "shard", None),
            P(None, ("expert", "shard"), None),
        ),
        out_specs=(
            P(None, ("expert", "shard"), None),
            P(None, ("expert", "shard"), None),
            P(("expert", "shard"), None),
            P(("expert", "shard"), None),
            P(("expert", "shard"), None),
            P(("expert", "shard")),
            P(("expert", "shard")),
            P(("expert", "shard")),
            P("expert", "shard", None),
            P("expert", "shard", None),
            P("expert", "shard", None),
        ),
        check_vma=False,
    )
```

```python
import functools

import jax
import jax.numpy as jnp
from jax import lax
from jax.experimental import pallas as pl
from jax.experimental.pallas import tpu as pltpu
from jax.sharding import PartitionSpec as P

HEAD = 128
EPS = 1e-06
ROPE_BASE = 10000.0
NEGATIVE = -1e30
LOW = jnp.bfloat16
F32 = jnp.float32


def rms_scale(values, gain_vec):
    return values * lax.rsqrt(jnp.mean(values * values, axis=-1, keepdims=True) + EPS) * gain_vec


def places(perm_row, length_row):
    seq_ends = jnp.cumsum(length_row)
    seg_ids = jnp.sum((perm_row[:, None] >= seq_ends[None, :]).astype(jnp.int32), axis=1)
    starts = seq_ends - length_row
    pick_mask = seg_ids[:, None] == jnp.arange(length_row.shape[0], dtype=jnp.int32)[None, :]
    seq_begin = jnp.sum(jnp.where(pick_mask, starts[None, :], 0), axis=1)
    return (seg_ids, perm_row - seq_begin)


def angles(positions):
    half_size = HEAD // 2
    frequency = jnp.power(ROPE_BASE, -2.0 * jnp.arange(half_size, dtype=F32) / HEAD)
    turned = positions.astype(F32)[..., None] * frequency
    cosine, sine = jnp.cos(turned), jnp.sin(turned)
    return (
        jnp.concatenate([cosine, cosine], axis=-1),
        jnp.concatenate([-sine, sine], axis=-1),
    )


def hop(value, axis, step):
    size = lax.axis_size(axis)
    return lax.ppermute(value, axis, [(i, i ^ step) for i in range(size)])


def gather_first(value, axis):
    size = lax.axis_size(axis)
    blocks = [None] * size
    blocks[0] = value
    for k in range(2, size, 2):
        blocks[k] = hop(value, axis, k)
    return blocks


def gather_second(blocks, axis):
    blocks = list(blocks)
    for k in range(0, len(blocks), 2):
        blocks[k + 1] = hop(blocks[k], axis, 1)
    return blocks


def gather_blocks(value, axis):
    return gather_second(gather_first(value, axis), axis)


def far_sum(half, received):
    return half[0].astype(F32) + sum(x.astype(F32) for x in received)


def near_sums(keep, received):
    return [(k.astype(F32) + r.astype(F32)).astype(LOW) for k, r in zip(keep, received)]


def far_sends(half, after):
    return [hop(tie(half[j], *after), "expert", 2 * j) for j in range(1, len(half))]


def scatter_blocks(blocks, axis):
    half = [
        (blocks[k].astype(F32) + hop(blocks[k + 1], axis, 1).astype(F32)).astype(LOW)
        for k in range(0, len(blocks), 2)
    ]
    return far_sum(half, [hop(half[j], axis, 2 * j) for j in range(1, len(half))])


def place_blocks(blocks, own, dim):
    size = blocks[0].shape[dim]
    shape = list(blocks[0].shape)
    shape[dim] = size * len(blocks)
    whole = jnp.zeros(shape, blocks[0].dtype)
    for k, block in enumerate(blocks):
        whole = lax.dynamic_update_slice_in_dim(whole, block, (own ^ k) * size, dim)
    return whole


def take_blocks(whole, own, count, dim):
    size = whole.shape[dim] // count
    return [lax.dynamic_slice_in_dim(whole, (own ^ k) * size, size, dim) for k in range(count)]


def swap(value, axis):
    return lax.all_to_all(value, axis, split_axis=0, concat_axis=0, tiled=True)


def dot(a, b):
    return jnp.dot(a, b, preferred_element_type=F32)


def ein(spec, a, b):
    return jnp.einsum(spec, a, b, preferred_element_type=F32)


def tie(value, *others):
    return lax.optimization_barrier((value, others))[0]


def mm(a, b, dims=((1,), (0,))):
    return lax.dot_general(a, b, (dims, ((), ())), preferred_element_type=F32)


def mm_nt(a, b):
    return mm(a, b, ((1,), (1,)))


def expert_kernel(n, tile, grads_near, shared, own_ref, *refs):
    refs = list(refs)

    def take(count):
        out = refs[:count]
        del refs[:count]
        return out

    near, (far_ref,) = take(n // 2), take(1)
    grads = take(n // 2 + 1) if grads_near else take(1)
    pick_ref, turned_ref, router_ref, gate_ref, up_ref, down_ref = take(6)
    take(shared)
    buffer_ref, d_result_ref, hidden_ref, dg_ref, du_ref, moe_ref = take(6)
    d_keep, d_send = take(2)
    acc_res, acc_db, grad_rows, gate_cols = take(4)
    own = own_ref[0]
    expert, step, steps = pl.program_id(0), pl.program_id(1), pl.num_programs(1)
    count = pl.num_programs(0)
    cap, rows = pick_ref.shape[3:]
    width = acc_res.shape[1]
    index = own * count + expert

    @pl.when(step == 0)
    def _():
        for k in range(n):
            span = pl.ds(k * cap, cap)
            block = far_ref[k // 2] if k % 2 else near[k // 2][...]
            pick = pick_ref[0, 0, own ^ k]
            buffer_ref[0, span, :] = mm(pick, block).astype(LOW)
            logits = mm_nt(router_ref[...], block)
            terms = jnp.exp(logits - jnp.max(logits, axis=0, keepdims=True))
            router = terms / jnp.sum(terms, axis=0, keepdims=True)
            lines = lax.broadcasted_iota(jnp.int32, router.shape, 0)
            row = jnp.sum(jnp.where(lines == index, router, 0.0), axis=0, keepdims=True)
            col = jnp.sum(pick.astype(F32) * row, axis=1, keepdims=True)
            if grads_near:
                block = grads[-1][k // 2] if k % 2 else grads[k // 2][...]
            else:
                block = grads[0][own ^ k]
            block = mm(pick, block)
            grad_rows[span, :] = block.astype(LOW)
            d_result_ref[0, span, :] = (col * block).astype(LOW)
            gate_cols[span, :] = jnp.broadcast_to(col, (cap, gate_cols.shape[1]))

    slots = n * cap
    for r in range(0, slots, tile):
        span = pl.ds(r, tile)
        rows_in = buffer_ref[0, span, :]
        gate_act = mm(rows_in, gate_ref[0])
        up_act = mm(rows_in, up_ref[0])
        d_hidden = mm_nt(d_result_ref[0, span, :], down_ref[0])
        sig = 1.0 / (1.0 + jnp.exp(-gate_act))
        silu = gate_act * sig
        hidden_ref[0, span, :] = (silu * up_act).astype(LOW)
        slope = sig * (1.0 + gate_act * (1.0 - sig))
        dg_ref[0, span, :] = (d_hidden * up_act * slope).astype(LOW)
        du_ref[0, span, :] = (d_hidden * silu).astype(LOW)

        @pl.when(step == 0)
        def _():
            acc_res[span, :] = mm(hidden_ref[0, span, :], down_ref[0])
            acc_db[span, :] = mm_nt(dg_ref[0, span, :], gate_ref[0]) + mm_nt(
                du_ref[0, span, :], up_ref[0]
            )

        @pl.when(step > 0)
        def _():
            acc_res[span, :] += mm(hidden_ref[0, span, :], down_ref[0])
            acc_db[span, :] += mm_nt(dg_ref[0, span, :], gate_ref[0]) + mm_nt(
                du_ref[0, span, :], up_ref[0]
            )

    @pl.when(step == steps - 1)
    def _():
        lines = count * n * rows // width
        place = index * rows
        line, column = place // width, place % width
        shape = (d_keep.shape[1] - rows, width)
        at_line = lax.broadcasted_iota(jnp.int32, shape, 0)
        at_column = lax.broadcasted_iota(jnp.int32, shape, 1)
        here = (at_column >= column) & (at_column < column + rows)
        for k in range(n):
            span = pl.ds(k * cap, cap)
            out = d_send if k % 2 else d_keep
            pick = pick_ref[0, 0, own ^ k]
            turned = turned_ref[0, 0, own ^ k]
            result = acc_res[span, :].astype(LOW).astype(F32)
            col = jnp.sum(result * grad_rows[span, :].astype(F32), axis=1, keepdims=True)
            row = jnp.sum(pick.astype(F32) * col, axis=0, keepdims=True)
            high = row.astype(LOW).astype(F32)
            high, rest = (
                jnp.concatenate([x] * (width // rows), axis=1) for x in (high, row - high)
            )
            extra = jnp.where(here & (at_line == line), high, 0.0) + jnp.where(
                here & (at_line == line + lines), rest, 0.0
            )
            part = mm(turned, (gate_cols[span, :1] * result).astype(LOW))
            d_part = mm(turned, acc_db[span, :].astype(LOW))

            @pl.when(expert == 0)
            def _():
                moe_ref[own ^ k, 0] = part.astype(LOW)
                out[k // 2, :rows] = d_part.astype(LOW)
                out[k // 2, rows:] = extra.astype(LOW)

            @pl.when(expert > 0)
            def _():
                moe_ref[own ^ k, 0] = (moe_ref[own ^ k, 0].astype(F32) + part).astype(LOW)
                out[k // 2, :rows] = (out[k // 2, :rows].astype(F32) + d_part).astype(LOW)
                out[k // 2, rows:] = (out[k // 2, rows:].astype(F32) + extra).astype(LOW)


def expert_layer(own, blocks, far, grads, pick, turned, router_turned, weights, at, micro, kept):
    n = 2 * len(blocks)
    rows, width = blocks[0].shape
    count, _, ff = weights[0].shape
    cap = pick.shape[3]
    slots = n * cap
    split = 2 if n <= 8 else 4
    ft = ff // split
    extra = 8
    one = dict(pipeline_mode=pl.Buffered(1))
    some = one if n > 8 else {}
    block = pl.BlockSpec((rows, width), lambda e, f, o: (0, 0), **one)

    def stack(size, height):
        return pl.BlockSpec((size, height, width), lambda e, f, o: (0, 0, 0), **one)

    row_block = pl.BlockSpec((1, slots, width), lambda e, f, o: (e, at, 0), **some)
    ff_block = pl.BlockSpec((1, slots, ft), lambda e, f, o: (e, at, f))
    rows_shape = jax.ShapeDtypeStruct((count, micro * slots, width), LOW)
    ff_shape = jax.ShapeDtypeStruct((count, micro * slots, ff), LOW)
    grads_near = len(grads) > 1
    kept = [] if kept is None else list(kept)
    args = [*blocks, far, *grads, pick, turned, router_turned, *weights]
    outs = pl.pallas_call(
        functools.partial(expert_kernel, n, 512, grads_near, len(kept)),
        out_shape=[rows_shape, rows_shape, ff_shape, ff_shape, ff_shape]
        + [jax.ShapeDtypeStruct((n, micro, rows, width), LOW)]
        + [jax.ShapeDtypeStruct((n // 2, rows + extra, width), LOW)] * 2,
        grid_spec=pltpu.PrefetchScalarGridSpec(
            num_scalar_prefetch=1,
            grid=(count, split),
            in_specs=[block] * (n // 2)
            + [stack(n // 2, rows)]
            + ([block] * (n // 2) + [stack(n // 2, rows)] if grads_near else [stack(n, rows)])
            + [
                pl.BlockSpec((1, 1, n, cap, rows), lambda e, f, o: (e, at, 0, 0, 0), **some),
                pl.BlockSpec((1, 1, n, rows, cap), lambda e, f, o: (e, at, 0, 0, 0), **some),
                pl.BlockSpec(router_turned.shape, lambda e, f, o: (0, 0)),
                pl.BlockSpec((1, width, ft), lambda e, f, o: (e, 0, f)),
                pl.BlockSpec((1, width, ft), lambda e, f, o: (e, 0, f)),
                pl.BlockSpec((1, ft, width), lambda e, f, o: (e, f, 0)),
            ]
            + [pl.BlockSpec(memory_space=pl.ANY)] * len(kept),
            out_specs=[row_block, row_block, ff_block, ff_block, ff_block]
            + [pl.BlockSpec((n, 1, rows, width), lambda e, f, o: (0, at, 0, 0), **one)]
            + [stack(n // 2, rows + extra)] * 2,
            scratch_shapes=[
                pltpu.VMEM((slots, width), F32),
                pltpu.VMEM((slots, width), F32),
                pltpu.VMEM((slots, width), LOW),
                pltpu.VMEM((slots, 128), F32),
            ],
        ),
        input_output_aliases={1 + len(args) + i: i for i in range(len(kept))},
        compiler_params=pltpu.CompilerParams(vmem_limit_bytes=60 << 20),
        cost_estimate=pl.CostEstimate(
            flops=24 * count * slots * width * ff,
            transcendentals=count * slots * ff,
            bytes_accessed=4 * n * rows * width * 2 + 3 * count * width * ff * 2,
        ),
        name="experts",
    )(own.reshape(1), *args, *kept)
    return outs[:6], outs[6], outs[7]


def turn(x):
    return pltpu.roll(x, HEAD // 2, 1)


def attend_kernel(n, tile, own_ref, *refs):
    xs = refs[:n]
    wq, wk, wv, gains_ref, cos_ref, sin_ref, seg_col, seg_row = refs[n : n + 8]
    attended_ref, normed_ref, raw_ref, low_ref = refs[-4:]
    own = own_ref[0]
    rows, width = xs[0].shape
    part = wq.shape[1]
    group = n * rows
    for k in range(n):
        normed_ref[own ^ k] = xs[k][...]
    for r in range(0, group, tile):
        span = pl.ds(r, tile)
        block = normed_ref[r // rows : (r + tile) // rows].reshape(tile, width)
        cos, sin = cos_ref[span, :], sin_ref[span, :]
        for which, weight in enumerate((wq, wk, wv)):
            out = mm(block, weight[...])
            if which == 2:
                low_ref[span, 2 * part :] = out.astype(LOW)
                continue
            raw_ref[span, which * part : (which + 1) * part] = out
            for h in range(part // HEAD):
                x = out[:, h * HEAD : (h + 1) * HEAD]
                x = x * lax.rsqrt(jnp.mean(x * x, axis=1, keepdims=True) + EPS)
                x = x * gains_ref[which : which + 1, :]
                x = x * cos + turn(x) * sin
                at = which * part + h * HEAD
                low_ref[span, at : at + HEAD] = x.astype(LOW)
    for h in range(part // HEAD):
        keys = low_ref[:, part + h * HEAD : part + (h + 1) * HEAD]
        values = low_ref[:, 2 * part + h * HEAD : 2 * part + (h + 1) * HEAD]
        for r in range(0, group, tile):
            query = low_ref[r : r + tile, h * HEAD : (h + 1) * HEAD]
            scores = mm_nt(query, keys) * HEAD**-0.5
            same = seg_col[r : r + tile, :] == seg_row[...]
            scores = jnp.where(same, scores, NEGATIVE)
            terms = jnp.exp(scores - jnp.max(scores, axis=1, keepdims=True))
            probs = terms * (1.0 / jnp.sum(terms, axis=1, keepdims=True))
            out = mm(probs.astype(LOW), values).astype(LOW)
            for i in range(0, tile, rows):
                attended_ref[(r + i) // rows, :rows, h * HEAD : (h + 1) * HEAD] = out[
                    i : i + rows
                ]
    if len(refs) > n + 12:
        for k in range(n):
            attended_ref[k, rows:, :] = refs[n + 8][...]


def attend(own, blocks, qkv_weight, gains, cos, sin, seg, riders, tile=512):
    n = len(blocks)
    rows, width = blocks[0].shape
    part = width // n
    group = n * rows
    more = sum(x.shape[0] for x in riders)

    def columns(which):
        return pl.BlockSpec((width, part), lambda i, o: (0, which * n + o[0]))

    def whole(*shape):
        return pl.BlockSpec(shape, lambda i, o: (0,) * len(shape))

    return pl.pallas_call(
        functools.partial(attend_kernel, n, tile),
        out_shape=[
            jax.ShapeDtypeStruct((n, rows + more, part), LOW),
            jax.ShapeDtypeStruct((n, rows, width), LOW),
            jax.ShapeDtypeStruct((group, 2 * part), F32),
            jax.ShapeDtypeStruct((group, 3 * part), LOW),
        ],
        grid_spec=pltpu.PrefetchScalarGridSpec(
            num_scalar_prefetch=1,
            grid=(1,),
            in_specs=[whole(rows, width)] * n
            + [columns(0), columns(1), columns(2)]
            + [
                whole(2, HEAD),
                whole(group, HEAD),
                whole(group, HEAD),
                whole(group, 1),
                whole(1, group),
            ]
            + [whole(*x.shape) for x in riders],
            out_specs=[
                whole(n, rows + more, part),
                whole(n, rows, width),
                whole(group, 2 * part),
                whole(group, 3 * part),
            ],
        ),
        compiler_params=pltpu.CompilerParams(vmem_limit_bytes=56 << 20),
        cost_estimate=pl.CostEstimate(
            flops=2 * group * (3 * width * part + 2 * group * part),
            transcendentals=group * group * (part // HEAD),
            bytes_accessed=group * (4 * width + 18 * part) + 6 * width * part,
        ),
        name="attend",
    )(
        own.reshape(1),
        *blocks,
        qkv_weight,
        qkv_weight,
        qkv_weight,
        gains,
        cos,
        sin,
        seg[:, None],
        seg[None, :],
        *riders,
    )


def attend_back_kernel(
    n,
    tile,
    d_ref,
    low_ref,
    raw_ref,
    gains_ref,
    cos_ref,
    sin_ref,
    seg_col,
    seg_row,
    out_ref,
    gain_ref,
    dq_ref,
    dk_ref,
    dv_ref,
):
    rows, part = d_ref.shape[1:]
    group = n * rows
    scale = HEAD**-0.5
    gain_terms = [jnp.zeros((1, HEAD), F32), jnp.zeros((1, HEAD), F32)]
    for h in range(part // HEAD):
        cols = slice(h * HEAD, (h + 1) * HEAD)
        keys = low_ref[:, part + h * HEAD : part + (h + 1) * HEAD]
        values = low_ref[:, 2 * part + h * HEAD : 2 * part + (h + 1) * HEAD]
        for r in range(0, group, tile):
            query = low_ref[r : r + tile, cols]
            d_out = d_ref[r // rows : (r + tile) // rows, :, cols].reshape(tile, HEAD)
            scores = mm_nt(keys, query) * scale
            same = seg_col[...] == seg_row[:, r : r + tile]
            scores = jnp.where(same, scores, NEGATIVE)
            terms = jnp.exp(scores - jnp.max(scores, axis=0, keepdims=True))
            probs = terms * (1.0 / jnp.sum(terms, axis=0, keepdims=True))
            d_probs = mm_nt(values, d_out)
            delta = jnp.sum(probs * d_probs, axis=0, keepdims=True)
            d_scores = (probs * (d_probs - delta)).astype(LOW)
            dv = mm(probs.astype(LOW), d_out)
            dk = mm(d_scores, query)
            dq_ref[r : r + tile, :] = mm(d_scores, keys, ((0,), (0,))) * scale
            if r == 0:
                dv_ref[...] = dv
                dk_ref[...] = dk * scale
            else:
                dv_ref[...] += dv
                dk_ref[...] += dk * scale
        for r in range(0, group, rows):
            span = pl.ds(r, rows)
            cos, sin = cos_ref[span, :], sin_ref[span, :]
            at = 2 * part + h * HEAD
            out_ref[r // rows, :, at : at + HEAD] = dv_ref[span, :].astype(LOW)
            for which, grad_ref in enumerate((dq_ref, dk_ref)):
                at = which * part + h * HEAD
                raw = raw_ref[span, at : at + HEAD]
                inv = lax.rsqrt(jnp.mean(raw * raw, axis=1, keepdims=True) + EPS)
                unit = raw * inv
                grad = grad_ref[span, :]
                grad = grad * cos + turn(grad * sin)
                gain_terms[which] += jnp.sum(grad * unit, axis=0, keepdims=True)
                grad = grad * gains_ref[which : which + 1, :]
                grad = inv * (grad - unit * jnp.mean(grad * unit, axis=1, keepdims=True))
                out_ref[r // rows, :, at : at + HEAD] = grad.astype(LOW)
    for which in range(2):
        gain_ref[which : which + 1, :] = gain_terms[which]


def attend_back(d_attended, low, raw, gains, cos, sin, seg, tile=512):
    n, rows, part = d_attended.shape
    group = n * rows
    return pl.pallas_call(
        functools.partial(attend_back_kernel, n, tile),
        out_shape=[
            jax.ShapeDtypeStruct((n, rows, 3 * part), LOW),
            jax.ShapeDtypeStruct((2, HEAD), F32),
        ],
        scratch_shapes=[pltpu.VMEM((group, HEAD), F32)] * 3,
        compiler_params=pltpu.CompilerParams(vmem_limit_bytes=56 << 20),
        cost_estimate=pl.CostEstimate(
            flops=10 * group * group * part,
            transcendentals=group * group * (part // HEAD),
            bytes_accessed=group * part * 22,
        ),
        name="attend_back",
    )(d_attended, low, raw, gains, cos, sin, seg[:, None], seg[None, :])


def local(
    tokens,
    cotangent,
    qkv_weight,
    out_weight,
    router_weight,
    attn_gain,
    moe_gain,
    head_gains,
    gate_weight,
    up_weight,
    down_weight,
    permutation,
    lengths,
    routes,
):
    micro, rows, width = tokens.shape
    n = lax.axis_size("expert")
    m = lax.axis_size("shard")
    own = lax.axis_index("expert")
    own_shard = lax.axis_index("shard")
    local_count = gate_weight.shape[0]
    expert_count = local_count * n
    top_count = routes.shape[2]
    capacity = rows * top_count // expert_count
    part = width // n
    piece = width // (n * m)

    full_gate = lax.all_gather(gate_weight, "shard", axis=1, tiled=True)
    full_up = lax.all_gather(up_weight, "shard", axis=1, tiled=True)
    full_down = lax.all_gather(down_weight, "shard", axis=1, tiled=True)

    each = range(micro)
    inputs = [tokens[i].astype(F32) for i in each]
    normed_attn = [rms_scale(x, attn_gain).astype(LOW) for x in inputs]
    near = [gather_first(normed_attn[0], "expert")]
    for i in range(1, micro):
        near.append(gather_first(tie(normed_attn[i], near[i - 1][2]), "expert"))
    gains = head_gains.reshape(2, HEAD)
    spots = [places(permutation[i, 0], lengths[i, 0]) for i in each]
    turns = [angles(pos) for _, pos in spots]
    normed_blocks = [gather_second(x, "expert") for x in near]
    grad_near = gather_first(tie(cotangent[0], *near[-1][2::2]), "expert")[::2]
    grad_far = hop(jnp.stack(grad_near), "expert", 1)
    grad_rest = [
        lax.all_gather(tie(cotangent[i], near[-1][-2]), "expert", axis=0) for i in range(1, micro)
    ]
    attended, normed_all, qkv_raw, qkv_low, mixed, normed_moe = ([None] * micro for _ in range(6))
    for i in each:
        riders = ()
        if i == 0:
            riders = (routes.astype(LOW).transpose(0, 2, 1).reshape(-1, part),)
        attended[i], normed_all[i], qkv_raw[i], qkv_low[i] = attend(
            own, normed_blocks[i], qkv_weight, gains, *turns[i], spots[i][0], riders
        )
        attended[i] = swap(attended[i], "expert")
        if i == 0:
            routes_all = attended[i][:, rows:]
            attended[i] = attended[i][:, :rows]
        elif i == 1:
            attended[i] = tie(attended[i], *grad_near[1:])
        mixed[i] = inputs[i] + ein("hrp,hpd->rd", attended[i], out_weight.reshape(n, part, width))
        normed_moe[i] = rms_scale(mixed[i], moe_gain).astype(LOW)
    attended_cols = jnp.stack([x.reshape(n, rows, m, piece) for x in attended])
    attended_cols = swap(attended_cols.transpose(3, 0, 2, 1, 4), "shard")
    attended_cols = attended_cols.reshape(m * micro * rows, n * piece)

    own_experts = own * local_count + jnp.arange(local_count, dtype=jnp.int32)
    by_micro = routes_all.reshape(n, micro, top_count, rows).swapaxes(0, 1).astype(jnp.int32)
    hit = jnp.any(by_micro[None] == own_experts[:, None, None, None, None], axis=3)
    hot = hit.astype(jnp.int32)
    slot = jnp.cumsum(hot, axis=-1) - hot
    slot_iota = jnp.arange(capacity, dtype=jnp.int32)
    pick = (hit[:, :, :, None, :] & (slot[:, :, :, None, :] == slot_iota[:, None])).astype(LOW)
    turned = (hit[..., None] & (slot[..., None] == slot_iota)).astype(LOW)

    weights = (full_gate, full_up, full_down)
    moe_near, moe_far = ([None] * micro for _ in range(2))
    for i in each:
        ready = tie(normed_moe[i], grad_far, *moe_near[i - 1][1:]) if i else normed_moe[i]
        moe_near[i] = gather_first(ready, "expert")[::2]
    moe_far[0] = jnp.stack([hop(x, "expert", 1) for x in moe_near[0]])
    grads = [(*grad_near, grad_far)] + [(x,) for x in grad_rest]
    kept, wait = None, (attended_cols, *moe_near[-1][1:])
    keep, received = ([None] * micro for _ in range(2))
    for i in each:
        if i:
            moe_far[i] = hop(jnp.stack(moe_near[i]), "expert", 1)
        kept, keep[i], send = expert_layer(
            own,
            [tie(moe_near[i][0], *wait)] + moe_near[i][1:],
            moe_far[i],
            grads[i],
            pick,
            turned,
            router_weight.T,
            weights,
            i,
            micro,
            kept,
        )
        received[i] = hop(send, "expert", 1)
        wait = ()
    buffer, d_result, hidden, dg, du, moe_sum = kept
    def grad_rows(term):
        return lax.psum_scatter(term, "shard", scatter_dimension=1, tiled=True)

    gate_term = ein("erd,erf->edf", buffer, dg).astype(LOW)
    up_term = ein("erd,erf->edf", buffer, tie(du, gate_term)).astype(LOW)
    half, far = [None] * micro, [None] * micro

    d_attn, d_attended, d_mixed, d_qkv, d_qkv_sent = ([None] * micro for _ in range(5))
    head_terms = [None] * micro
    router_term, moe_gain_term = 0.0, 0.0
    for i in each:
        half[i] = near_sums(
            keep[i], tie(received[i], *(d_attn[i - 1],) if i else (buffer,))
        )
        far[i] = far_sends(half[i], ())
        if i:
            gate_grad = lax.psum_scatter(
                tie(gate_term, half[i][0]), "shard", scatter_dimension=1, tiled=True
            )
        total = far_sum(half[i], far[i])
        if i == 0:
            total = tie(total, gate_term)
        if i:
            down_term = ein("erf,erd->efd", tie(hidden, half[i][0]), d_result).astype(LOW)
            total = tie(total, up_term)
        d_normed = total[:rows]
        lines = expert_count * rows // width
        d_router = total[rows : rows + lines] + total[rows + lines : rows + 2 * lines]
        d_router = d_router.reshape(expert_count, rows).T
        grad_out = cotangent[i].astype(F32)
        logits = dot(normed_moe[i], router_weight)
        exp_logits = jnp.exp(logits - jnp.max(logits, axis=-1, keepdims=True))
        router = exp_logits / jnp.sum(exp_logits, axis=-1, keepdims=True)
        d_logits = (
            router * (d_router - jnp.sum(router * d_router, axis=-1, keepdims=True))
        ).astype(LOW)
        d_normed = d_normed + dot(d_logits, router_weight.T)
        router_term = router_term + dot(normed_moe[i].T, d_logits)
        _, norm_pull = jax.vjp(rms_scale, mixed[i], moe_gain)
        d_mixed_norm, term = norm_pull(d_normed)
        moe_gain_term = moe_gain_term + term
        d_mixed[i] = grad_out + d_mixed_norm
        d_attn[i] = d_mixed[i].astype(LOW)
        back = dot(d_attn[i], out_weight.T).astype(LOW)
        back = jnp.swapaxes(back.reshape(rows, n, part), 0, 1)
        d_attended[i] = swap(back, "expert")
        d_qkv[i], head_terms[i] = attend_back(
            d_attended[i], qkv_low[i], qkv_raw[i], gains, *turns[i], spots[i][0]
        )
        d_qkv_sent[i] = swap(d_qkv[i], "expert")

    moe_part = lax.psum_scatter(
        tie(moe_sum, d_attended[-1]).reshape(n * micro * rows, width),
        "expert",
        scatter_dimension=0,
        tiled=True,
    ).reshape(micro, rows, width)

    up_grad = scatter_blocks(take_blocks(tie(up_term, d_qkv[-1]), own_shard, m, 1), "shard")

    down_grad = scatter_blocks(
        take_blocks(tie(down_term, d_qkv[-1]), own_shard, m, 1), "shard"
    )

    d_attn_all = place_blocks(
        gather_blocks(tie(jnp.concatenate(d_attn, axis=0), d_qkv[-1]), "shard"), own_shard, 0
    )
    out_term = dot(tie(attended_cols, d_qkv[-1]).T, d_attn_all)
    out_term = out_term.astype(LOW)
    parts = take_blocks(out_term, own, n, 0)
    out_near = hop(jnp.stack(parts[1::2]), "expert", 1)
    out_half = near_sums(parts[::2], out_near)
    out_grad = far_sum(out_half, far_sends(out_half, ()))
    head_term = sum(head_terms).reshape(2 * HEAD)

    def input_gradient(i, *wait):
        sent = d_qkv_sent[i].reshape(n, rows, 3, part).transpose(1, 2, 0, 3)
        d_normed_attn = dot(tie(sent.reshape(rows, 3 * width), *wait), qkv_weight.T)
        _, pull = jax.vjp(lambda x: rms_scale(x, attn_gain), inputs[i])
        return (d_mixed[i] + pull(d_normed_attn)[0]).astype(LOW)

    qkv_term = sum(
        dot(normed_all[i].reshape(n * rows, width).T, d_qkv[i].reshape(n * rows, 3 * part))
        for i in reversed(each)
    ).astype(LOW)
    qkv_term = jnp.swapaxes(qkv_term.reshape(n, m, piece, 3 * part), 0, 1)
    parts = take_blocks(qkv_term, own_shard, m, 0)
    qkv_half = [
        (parts[k].astype(F32) + hop(parts[k + 1], "shard", 1).astype(F32)).astype(LOW)
        for k in range(0, m, 2)
    ]
    qkv_far = [hop(qkv_half[j], "shard", 2 * j) for j in range(1, m // 2)]
    gate_grad, up_grad, down_grad = (x.astype(F32) for x in (gate_grad, up_grad, down_grad))
    input_grad = [input_gradient(i, qkv_half[0]) for i in range(micro - 1)]
    qkv_sum = far_sum(qkv_half, qkv_far).astype(LOW)
    qkv_sum = tie(qkv_sum, d_qkv_sent[-1], *input_grad)
    qkv_rows = swap(qkv_sum.reshape(n, piece, 3 * part), "expert")
    qkv_grad = (
        qkv_rows.reshape(n, piece, 3, part).transpose(1, 2, 0, 3).reshape(piece, 3 * width)
    ).astype(F32)
    input_grad.append(input_gradient(micro - 1, qkv_sum))
    output = [(mixed[i] + moe_part[i].astype(F32)).astype(LOW) for i in each]
    output, input_grad = jnp.stack(output), jnp.stack(input_grad)

    first = (own * m + own_shard) * piece
    own_rows = lax.dynamic_slice_in_dim(qkv_weight, first, piece, 0).astype(F32)
    own_gain = lax.dynamic_slice_in_dim(attn_gain, first, piece, 0)
    attn_gain_grad = jnp.sum(qkv_grad * own_rows, axis=1) / own_gain

    world = n * m
    head_piece = 2 * HEAD // world
    small = jnp.concatenate(
        [
            router_term.reshape(world, piece * expert_count),
            moe_gain_term.reshape(world, piece),
            head_term.reshape(world, head_piece),
        ],
        axis=1,
    )
    used = small.shape[1]
    padded = -(-used // 1024) * 1024
    small = jnp.pad(small, ((0, 0), (0, padded - used))).reshape(world, padded // 128, 128)
    small = tie(small, d_qkv_sent[-1])
    small = jnp.sum(swap(small, ("expert", "shard")), axis=0).reshape(padded)
    a = piece * expert_count
    return (
        output,
        input_grad,
        qkv_grad,
        out_grad,
        small[:a].reshape(piece, expert_count),
        attn_gain_grad,
        small[a : a + piece],
        small[a + piece : a + piece + head_piece],
        gate_grad,
        up_grad,
        down_grad,
    )


def solution(mesh):
    return jax.shard_map(
        local,
        mesh=mesh,
        in_specs=(
            P(None, ("expert", "shard"), None),
            P(None, ("expert", "shard"), None),
            P(),
            P(),
            P(),
            P(),
            P(),
            P(),
            P("expert", "shard", None),
            P("expert", "shard", None),
            P("expert", "shard", None),
            P(None, "shard", None),
            P(None, "shard", None),
            P(None, ("expert", "shard"), None),
        ),
        out_specs=(
            P(None, ("expert", "shard"), None),
            P(None, ("expert", "shard"), None),
            P(("expert", "shard"), None),
            P(("expert", "shard"), None),
            P(("expert", "shard"), None),
            P(("expert", "shard")),
            P(("expert", "shard")),
            P(("expert", "shard")),
            P("expert", "shard", None),
            P("expert", "shard", None),
            P("expert", "shard", None),
        ),
        check_vma=False,
    )
```
